32 devices in a mesh: src: 2 (over core), brick: 16 (over z, y, x).
Axes of the slice: x: 2, y: 2, z: 4, core: 2. Of those that a mesh axis runs over, the one named last changes fastest.
Arguments:
- slowness: float32 [64, 64, 128], P('brick'), may hold values from 0.5 to 2
- source_x: int32 [4], P('src'), may hold values from 0 to 63
- source_y: int32 [4], P('src'), may hold values from 0 to 63
- source_z: int32 [4], P('src'), may hold values from 0 to 127
- station_x: int32 [2048], replicated, may hold values from 0 to 63
- station_y: int32 [2048], replicated, may hold values from 0 to 63
- station_z: int32 [2048], replicated, may hold values from 0 to 127
- observed: float32 [4, 2048], P('src'), may hold values from 0 to 4
Outputs:
- kernel: float32 [64, 64, 128], P('brick', 'src')
- arrivals: float32 [4, 2048], P('src', 'brick')
The draws below stay inside these ranges and needn't reach their ends.
All inputs are finite; a program needn't handle non-finite values.
Results may differ from the reference program's by a relative error of at most 0.0003.
Values sent between devices are 32-bit elements; how exact they have to be, the bound alone decides.
A program may use at most 128 MiB of HBM per device.

```python
import math
import jax
import jax.numpy as jnp
from jax import lax

NY = 64
NZ = 128
REC = 2048
ITERS = 16
NX = 64
SOURCES = 4


def touch_ends(values, key, low, high):
    extent = values.shape
    spot = [jax.random.randint(jax.random.fold_in(key, axis), (), 0, extent[axis]) for axis in range(len(extent))]
    values = values.at[tuple(spot)].set(low)
    longest = extent.index(max(extent))
    spot[longest] = (spot[longest] + 1) % extent[longest]
    return values.at[tuple(spot)].set(high)


def steps_of(key, extent, shards, low, largest):
    def one(position, parts):
        draws = jax.random.uniform(jax.random.fold_in(jax.random.fold_in(key, 6), position), (parts,), jnp.float32, low / len(shards), largest / len(shards))
        return jnp.repeat(jnp.exp(draws), extent[position] // parts).reshape((-1,) + (1,) * (len(extent) - position - 1))

    loudness = one(*shards[0])
    for cut in shards[1:]:
        loudness = loudness * one(*cut)
    return loudness


def setup_inputs(seed: int = 0) -> dict:
    key_list = jax.random.split(jax.random.key(seed), 9)
    return {
        "slowness": jnp.clip(jnp.exp(math.log(2.0) - 1.3862944 * jax.random.uniform(key_list[0], (NX, NY, NZ), jnp.float32) ** steps_of(key_list[0], (NX, NY, NZ), ((0, 16),), -0.2, 0.2)), 0.5, 2.0),
        "source_x": touch_ends(jax.random.randint(key_list[1], (SOURCES,), 0, NX), jax.random.fold_in(key_list[1], 1), 0, NX - 1).astype(jnp.int32),
        "source_y": touch_ends(jax.random.randint(key_list[2], (SOURCES,), 0, NY), jax.random.fold_in(key_list[2], 1), 0, NY - 1).astype(jnp.int32),
        "source_z": touch_ends(jax.random.randint(key_list[3], (SOURCES,), 0, NZ), jax.random.fold_in(key_list[3], 1), 0, NZ - 1).astype(jnp.int32),
        "station_x": touch_ends(jax.random.randint(key_list[4], (REC,), 0, NX), jax.random.fold_in(key_list[4], 1), 0, NX - 1).astype(jnp.int32),
        "station_y": touch_ends(jax.random.randint(key_list[5], (REC,), 0, NY), jax.random.fold_in(key_list[5], 1), 0, NY - 1).astype(jnp.int32),
        "station_z": touch_ends(jax.random.randint(key_list[6], (REC,), 0, NZ), jax.random.fold_in(key_list[6], 1), 0, NZ - 1).astype(jnp.int32),
        "observed": jnp.clip(4.0 * jax.random.uniform(key_list[7], (SOURCES, REC), jnp.float32) ** steps_of(key_list[7], (SOURCES, REC), ((0, 2),), -0.2, 0.2), 0.0, 4.0),
    }


spacing = 0.015625
big_value = 1000000.0
start_slowness = 2.0

def neighbours(padded):
    return [padded[2:, 1:-1, 1:-1], padded[:-2, 1:-1, 1:-1], padded[1:-1, 2:, 1:-1], padded[1:-1, :-2, 1:-1], padded[1:-1, 1:-1, 2:], padded[1:-1, 1:-1, :-2]]

def reference(slowness, source_x, source_y, source_z, station_x, station_y, station_z, observed):
    slow_pad = jnp.pad(slowness, 1, constant_values=1.0)
    costs = [spacing * 0.5 * (slowness + other) for other in neighbours(slow_pad)]
    grid_x = jnp.arange(NX, dtype=jnp.float32)[:, None, None]
    grid_y = jnp.arange(NY, dtype=jnp.float32)[None, :, None]
    grid_z = jnp.arange(NZ, dtype=jnp.float32)[None, None, :]
    flat = ((station_x * NY + station_y) * NZ + station_z).astype(jnp.int32)

    def forward_sweep(step, times):
        padded = jnp.pad(times, 1, constant_values=big_value)
        fresh = times
        for cost, other in zip(costs, neighbours(padded)):
            fresh = jnp.minimum(fresh, other + cost)
        return fresh

    def one_source(total, inputs):
        sx, sy, sz, seen = inputs
        dist = (grid_x - sx.astype(jnp.float32)) ** 2 + (grid_y - sy.astype(jnp.float32)) ** 2 + (grid_z - sz.astype(jnp.float32)) ** 2
        times = start_slowness * spacing * jnp.sqrt(dist)
        times = lax.fori_loop(0, ITERS, forward_sweep, times)
        arrive = times.reshape(-1)[flat]
        source = jnp.zeros((NX * NY * NZ,), jnp.float32).at[flat].add(arrive - seen).reshape(NX, NY, NZ)
        low_pad = jnp.pad(times, 1, constant_values=-big_value)
        weights = [jnp.maximum(other - times, 0.0) / spacing for other in neighbours(low_pad)]
        denom = 1.0 + weights[0] + weights[1] + weights[2] + weights[3] + weights[4] + weights[5]

        def adjoint_sweep(step, field):
            padded = jnp.pad(field, 1)
            acc = source
            for weight, other in zip(weights, neighbours(padded)):
                acc = acc + weight * other
            return acc / denom
        field = lax.fori_loop(0, ITERS, adjoint_sweep, jnp.zeros((NX, NY, NZ), jnp.float32))
        return (total + field, arrive)
    summed, arrivals = lax.scan(one_source, jnp.zeros((NX, NY, NZ), jnp.float32), (source_x, source_y, source_z, observed))
    return (slowness * summed, arrivals)
```

```python
import functools

import jax
import jax.numpy as jnp
from jax import lax
from jax.experimental import pallas as pl
from jax.experimental.pallas import tpu as pltpu
from jax.sharding import PartitionSpec as P

ITERS = 16

spacing = 0.015625
big_value = 1000000.0
start_slowness = 2.0
half_step = 0.5 * spacing
LOW = 4

VMEM = pl.BlockSpec(memory_space=pltpu.VMEM)
SMEM = pl.BlockSpec(memory_space=pltpu.SMEM)
MESH = pl.DeviceIdType.MESH


def remote(src, dst, send_sem, recv_sem, core, brick):
    return pltpu.make_async_remote_copy(
        src_ref=src,
        dst_ref=dst,
        send_sem=send_sem,
        recv_sem=recv_sem,
        device_id={"src": core, "brick": brick},
        device_id_type=MESH,
    )


def gather_kernel(bricks, slow_ref, full_ref, send_sem, recv_sem, twin_sem, own_sem):
    depth = slow_ref.shape[0]
    half = depth // 2
    lines = bricks // LOW
    me = lax.axis_index("brick")
    core = lax.axis_index("src")
    h = lax.rem(core, 2)
    twin = core + 1 - 2 * h
    line = me // LOW
    bit_x = lax.rem(me, 2)
    bit_y = lax.rem(me // 2, 2)
    flip_x = 1 - 2 * bit_x
    flip_y = 2 - 4 * bit_y
    first = me + flip_x * (1 - h) + flip_y * h
    second = me + flip_y * (1 - h) + flip_x * h
    corner = me + flip_x + flip_y
    has_down = line > 0
    has_up = line < lines - 1

    def piece(q, part):
        return full_ref.at[pl.ds(q * depth + part * half, half)]

    def copy(kind, q, brick, own=False):
        src = slow_ref.at[pl.ds(h * half, half)] if own else piece(q, h)
        return remote(src, piece(q, h), send_sem.at[kind, q], recv_sem.at[q], core, brick)

    def twin_copy(q):
        return remote(piece(q, h), piece(q, h), send_sem.at[4, q], twin_sem.at[q], twin, me)

    barrier = pltpu.get_barrier_semaphore()

    def greet(c, b):
        pl.semaphore_signal(barrier, inc=1, device_id={"src": c, "brick": b}, device_id_type=MESH)

    greet(twin, me)
    greet(core, first)
    greet(core, second)
    pl.when(has_down)(lambda: greet(core, me - LOW))
    pl.when(has_up)(lambda: greet(core, me + LOW))
    pl.semaphore_wait(barrier, 3 + has_down.astype(jnp.int32) + has_up.astype(jnp.int32))

    def sends(q, own, to_down, to_up, wait):
        def go(c):
            c.wait_send() if wait else c.start()

        if to_down is not None:
            pl.when(to_down)(lambda: go(copy(0, q, me - LOW, own)))
        if to_up is not None:
            pl.when(to_up)(lambda: go(copy(1, q, me + LOW, own)))
        go(copy(2, q, first, own))
        go(copy(3, q, second, own))

    own_copy = pltpu.make_async_copy(slow_ref, full_ref.at[pl.ds(me * depth, depth)], own_sem)
    sends(me, True, has_down, has_up, False)
    own_copy.start()

    def arrived(q):
        remote(piece(q, h), piece(q, h), send_sem.at[0, q], recv_sem.at[q], core, first).wait_recv()

    def on_line(base, i, act):
        pl.when((i < lines) & (line >= i))(lambda: act(base - LOW * i, -1))
        pl.when((i < lines) & (line + i < lines))(lambda: act(base + LOW * i, 1))

    def both(base, i, act):
        pl.when(i == 0)(lambda: act(base, 0))
        pl.when(i > 0)(lambda: on_line(base, i, act))

    def from_line(wait):
        def act(q, side):
            if not wait:
                arrived(q)
            sends(q, False, has_down if side > 0 else None, has_up if side < 0 else None, wait)
            c = twin_copy(q)
            c.wait_send() if wait else c.start()

        return act

    def from_first(wait):
        def act(q, side):
            if not wait:
                arrived(q)
            c = copy(3, q, second)
            c.wait_send() if wait else c.start()
            c = twin_copy(q)
            c.wait_send() if wait else c.start()

        return act

    def from_second(wait):
        def act(q, side):
            if not wait:
                arrived(q)
            c = twin_copy(q)
            c.wait_send() if wait else c.start()

        return act

    def turn(i, wait):
        on_line(me, i, from_line(wait))
        both(first, i - 1, from_first(wait))
        both(second, i - 1, from_second(wait))
        pl.when(i >= 2)(lambda: both(corner, i - 2, from_second(wait)))

    @pl.loop(1, lines + 2)
    def _(i):
        turn(i, False)

    own_copy.wait()
    sends(me, True, has_down, has_up, True)

    @pl.loop(1, lines + 2)
    def _(i):
        turn(i, True)

    @pl.loop(0, bricks)
    def _(q):
        @pl.when(q != me)
        def _():
            remote(piece(q, 1 - h), piece(q, 1 - h), send_sem.at[4, q], twin_sem.at[q], twin, me).wait_recv()


def window(pair_depth, grid_x, margin):
    length = min(grid_x, pair_depth + 2 * margin)
    pair = lax.axis_index("brick") // 2
    return jnp.clip(pair * pair_depth - margin, 0, grid_x - length), length


def stations_kernel(grid_x, cells_y, pair_depth, stx_ref, sty_ref, stz_ref, obs_ref, cnt_ref, sum_ref, table):
    rec = stx_ref.shape[1]
    cells_z = cnt_ref.shape[2]
    rows_y = cells_y // 8
    shift = rows_y.bit_length() - 1
    low, length = window(pair_depth, grid_x, ITERS)
    parity = lax.rem(lax.axis_index("brick"), 2)
    sty = sty_ref[...]
    row = (stx_ref[...] - low) * cells_y + (sty & (rows_y - 1)) * 8 + (sty >> shift)
    seen = obs_ref[pl.ds(parity, 1), :]
    hi = seen.astype(jnp.bfloat16).astype(jnp.float32)
    rest = seen - hi
    mid = rest.astype(jnp.bfloat16).astype(jnp.float32)
    lo = rest - mid
    hit = lax.broadcasted_iota(jnp.int32, (cells_z, rec), 0) == stz_ref[...]
    for part, value in enumerate((jnp.ones_like(seen), hi, mid, lo)):
        table[pl.ds(part * cells_z, cells_z), :] = jnp.where(hit, value, 0.0).astype(jnp.bfloat16)
    block = 256
    tiles = block // 8

    @pl.loop(0, length * cells_y // block)
    def _(step):
        rows = lax.broadcasted_iota(jnp.int32, (block, rec), 0) + step * block
        pick = jnp.where(rows == row, 1.0, 0.0).astype(jnp.bfloat16)
        got = lax.dot_general(
            pick, table[...], (((1,), (1,)), ((), ())), preferred_element_type=jnp.float32
        )
        cnt_ref[pl.ds(step * tiles, tiles)] = got[:, :cells_z].reshape(tiles, 8, cells_z)
        total = got[:, cells_z : 2 * cells_z] + (
            got[:, 2 * cells_z : 3 * cells_z] + got[:, 3 * cells_z :]
        )
        sum_ref[pl.ds(step * tiles, tiles)] = total.reshape(tiles, 8, cells_z)


def solve_kernel(
    pair_depth,
    sx_ref,
    sy_ref,
    sz_ref,
    stx_ref,
    sty_ref,
    stz_ref,
    slow_ref,
    cnt_ref,
    sum_ref,
    adj_ref,
    arr_ref,
    time,
    cost,
    picked,
    weight,
    supply,
    field,
):
    grid_x, cells_y, cells_z = slow_ref.shape
    rows = cells_y // 8
    shift = rows.bit_length() - 1
    brick = lax.axis_index("brick")
    parity = lax.rem(brick, 2)
    pair = brick // 2
    lane = lax.broadcasted_iota(jnp.int32, (8, cells_z), 1)
    sub = lax.broadcasted_iota(jnp.int32, (8, cells_z), 0)
    lane_first = lane == 0
    lane_last = lane == cells_z - 1
    sub_first = sub == 0
    sub_last = sub == 7

    def layer_of(ref, x):
        return tuple(ref[x * rows + v] for v in range(rows))

    def y_up(cur, v):
        return cur[v + 1] if v + 1 < rows else pltpu.roll(cur[0], 7, 0)

    def y_down(cur, v):
        return cur[v - 1] if v else pltpu.roll(cur[rows - 1], 1, 0)

    def z_up(one):
        return pltpu.roll(one, cells_z - 1, 1)

    def z_down(one):
        return pltpu.roll(one, 1, 1)

    sx = sx_ref[parity]
    sy = sy_ref[parity]
    sz = sz_ref[parity]
    dz = (lane - sz).astype(jnp.float32)
    flat = []
    for v in range(rows):
        dy = (sub * rows + v - sy).astype(jnp.float32)
        flat.append(dy * dy + dz * dz)

    @pl.loop(0, grid_x)
    def _(x):
        dx = (x - sx).astype(jnp.float32)
        for v in range(rows):
            slow = slow_ref[x, pl.ds(v, 8, stride=rows), :]
            start = (start_slowness * spacing) * jnp.sqrt(dx * dx + flat[v])
            cost[x * rows + v] = (2.0 * half_step) * slow
            time[(x + 1) * rows + v] = start + half_step * slow

    def pads(value):
        for v in range(rows):
            time[v] = jnp.full((8, cells_z), value, jnp.float32)
            time[(grid_x + 1) * rows + v] = jnp.full((8, cells_z), value, jnp.float32)

    pads(big_value)
    group = 2

    def forward(x, prev, cur):
        nxt = layer_of(time, x + 2)
        for v in range(rows):
            one = cur[v]
            up = y_up(cur, v)
            down = y_down(cur, v)
            if v + 1 == rows:
                up = jnp.where(sub_last, big_value, up)
            if v == 0:
                down = jnp.where(sub_first, big_value, down)
            ahead = jnp.where(lane_last, big_value, z_up(one))
            behind = jnp.where(lane_first, big_value, z_down(one))
            low = jnp.minimum(
                jnp.minimum(jnp.minimum(prev[v], nxt[v]), jnp.minimum(up, down)), jnp.minimum(ahead, behind)
            )
            time[(x + 1) * rows + v] = jnp.minimum(one, low + cost[x * rows + v])
        return nxt

    @pl.loop(0, ITERS)
    def _(sweep):
        def body(i, carry):
            prev, cur = carry
            for j in range(group):
                nxt = forward(i * group + j, prev, cur)
                prev, cur = cur, nxt
            return prev, cur

        lax.fori_loop(0, grid_x // group, body, (layer_of(time, 0), layer_of(time, 1)))

    @pl.loop(0, grid_x)
    def _(x):
        for v in range(rows):
            time[(x + 1) * rows + v] = time[(x + 1) * rows + v] - 0.5 * cost[x * rows + v]

    pads(-big_value)

    count = picked.shape[0]
    line = lax.broadcasted_iota(jnp.int32, (1, cells_z), 1)
    unroll = 8

    @pl.loop(0, count // unroll)
    def _(i):
        for j in range(unroll):
            r = pair * count + i * unroll + j
            y = sty_ref[r]
            at = (stx_ref[r] + 1) * rows + (y & (rows - 1))
            got = time[at, pl.ds(y >> shift, 1), :]
            picked[pl.ds(i * unroll + j, 1), :] = jnp.where(line == stz_ref[r], got, 0.0)

    arrived = jnp.sum(jnp.transpose(picked[...]), axis=0, keepdims=True)
    arr_ref[0] = arrived[:, : count // 2]
    arr_ref[1] = arrived[:, count // 2 :]

    base, length = window(pair_depth, grid_x, ITERS - 1)
    outer, _ = window(pair_depth, grid_x, ITERS)

    def weigh(x, prev, cur):
        nxt = layer_of(time, x + 2)
        spot = (x - base) * rows
        for v in range(rows):
            one = cur[v]

            def gain(other):
                return jnp.maximum(other - one, 0.0)

            up = gain(y_up(cur, v))
            down = gain(y_down(cur, v))
            if v + 1 == rows:
                up = jnp.where(sub_last, 0.0, up)
            if v == 0:
                down = jnp.where(sub_first, 0.0, down)
            parts = (
                gain(prev[v]),
                gain(nxt[v]),
                down,
                up,
                jnp.where(lane_first, 0.0, gain(z_down(one))),
                jnp.where(lane_last, 0.0, gain(z_up(one))),
            )
            total = ((parts[0] + parts[1]) + (parts[2] + parts[3])) + (parts[4] + parts[5])
            inverse = 1.0 / (1.0 + total * (1.0 / spacing))
            scaled = inverse * (1.0 / spacing)
            for k, part in enumerate(parts):
                weight[k, spot + v] = part * scaled
            here = (x - outer) * rows + v
            value = (cnt_ref[here] * one - sum_ref[here]) * inverse
            supply[spot + v] = value
            field[spot + rows + v] = value
        return nxt

    def weigh_body(i, carry):
        prev, cur = carry
        for j in range(group):
            nxt = weigh(base + i * group + j, prev, cur)
            prev, cur = cur, nxt
        return prev, cur

    lax.fori_loop(0, length // group, weigh_body, (layer_of(time, base), layer_of(time, base + 1)))
    for v in range(rows):
        field[v] = jnp.zeros((8, cells_z), jnp.float32)
        field[(length + 1) * rows + v] = jnp.zeros((8, cells_z), jnp.float32)

    def backward(x, prev, cur):
        nxt = layer_of(field, x + 2)
        for v in range(rows):
            one = cur[v]
            spot = x * rows + v
            acc = supply[spot] + weight[0, spot] * prev[v]
            acc = acc + weight[1, spot] * nxt[v]
            side = weight[2, spot] * y_down(cur, v) + weight[3, spot] * y_up(cur, v)
            acc = acc + side
            acc = acc + (weight[4, spot] * z_down(one) + weight[5, spot] * z_up(one))
            field[spot + rows] = acc
        return nxt

    @pl.loop(2, ITERS + 1)
    def _(sweep):
        margin = ITERS - sweep
        span = jnp.minimum(grid_x, pair_depth + 2 * margin)
        first = jnp.clip(pair * pair_depth - margin, 0, grid_x - span) - base

        def body(i, carry):
            prev, cur = carry
            for j in range(group):
                nxt = backward(first + i * group + j, prev, cur)
                prev, cur = cur, nxt
            return prev, cur

        lax.fori_loop(0, span // group, body, (layer_of(field, first), layer_of(field, first + 1)))

    mine = pair * pair_depth - base + 1
    for x in range(pair_depth):
        for v in range(rows):
            adj_ref[x, pl.ds(v, 8, stride=rows), :] = field[(mine + x) * rows + v]


def reduce_kernel(cores, adj_ref, arr_ref, out_ref, got_ref, slots, send_sem, recv_sem, word_send, word_recv):
    depth, keep, _ = out_ref.shape
    brick = lax.axis_index("brick")
    core = lax.axis_index("src")
    parity = lax.rem(brick, 2)
    other = brick + 1 - 2 * parity
    me = core * 2 + parity

    def target(k):
        c = lax.rem(core + k // 2, cores)
        p = lax.rem(parity + k % 2, 2)
        return c, p, brick - parity + p

    def copy(k):
        c, p, b = target(k)
        return remote(
            adj_ref.at[pl.ds(p * depth, depth), pl.ds(c * keep, keep)],
            slots.at[k],
            send_sem.at[k],
            recv_sem.at[k],
            c,
            b,
        )

    barrier = pltpu.get_barrier_semaphore()
    for k in range(1, 2 * cores):
        c, _, b = target(k)
        pl.semaphore_signal(barrier, inc=1, device_id={"src": c, "brick": b}, device_id_type=MESH)
    pl.semaphore_wait(barrier, 2 * cores - 1)
    word = remote(arr_ref.at[1 - parity], got_ref.at[parity], word_send, word_recv, core, other)
    word.start()
    for k in range(1, 2 * cores):
        copy(k).start()
    got_ref[parity] = arr_ref[parity]
    total = adj_ref[pl.ds(parity * depth, depth), pl.ds(pl.multiple_of(core * keep, 8), keep), :]
    for k in range(1, 2 * cores):
        copy(k).wait_recv()
        total = total + slots[k]
    out_ref[...] = total
    for k in range(1, 2 * cores):
        copy(k).wait_send()
    word.wait_send()
    remote(arr_ref.at[parity], got_ref.at[1 - parity], word_send, word_recv, core, other).wait_recv()


def per_device(slowness, source_x, source_y, source_z, station_x, station_y, station_z, observed):
    bricks = lax.axis_size("brick")
    cores = lax.axis_size("src")
    depth, cells_y, cells_z = slowness.shape
    grid_x = depth * bricks
    rec = station_x.shape[0]
    pair_depth = 2 * depth
    rows = cells_y // 8
    assert source_x.shape[0] == 2 and bricks % LOW == 0 and cores % 2 == 0
    f32 = jnp.float32

    full = pl.pallas_call(
        functools.partial(gather_kernel, bricks),
        name="gather",
        out_shape=jax.ShapeDtypeStruct((grid_x, cells_y, cells_z), f32),
        in_specs=[VMEM],
        out_specs=VMEM,
        scratch_shapes=[
            pltpu.SemaphoreType.DMA((5, bricks)),
            pltpu.SemaphoreType.DMA((bricks,)),
            pltpu.SemaphoreType.DMA((bricks,)),
            pltpu.SemaphoreType.DMA,
        ],
        compiler_params=pltpu.CompilerParams(collective_id=0, has_side_effects=True),
    )(slowness)

    wide = min(grid_x, pair_depth + 2 * ITERS)
    field = jax.ShapeDtypeStruct((wide * rows, 8, cells_z), f32)
    cnt, total = pl.pallas_call(
        functools.partial(stations_kernel, grid_x, cells_y, pair_depth),
        name="stations",
        out_shape=(field, field),
        in_specs=[VMEM] * 4,
        out_specs=(VMEM, VMEM),
        scratch_shapes=[pltpu.VMEM((4 * cells_z, rec), jnp.bfloat16)],
    )(station_x[None], station_y[None], station_z[None], observed)

    length = min(grid_x, pair_depth + 2 * (ITERS - 1))
    share = rec // bricks
    adj, arr = pl.pallas_call(
        functools.partial(solve_kernel, pair_depth),
        name="solve",
        out_shape=(
            jax.ShapeDtypeStruct((pair_depth, cells_y, cells_z), f32),
            jax.ShapeDtypeStruct((2, 1, share), f32),
        ),
        in_specs=[SMEM] * 6 + [VMEM] * 3,
        out_specs=(VMEM, VMEM),
        scratch_shapes=[
            pltpu.VMEM(((grid_x + 2) * rows, 8, cells_z), f32),
            pltpu.VMEM((grid_x * rows, 8, cells_z), f32),
            pltpu.VMEM((2 * share, cells_z), f32),
            pltpu.VMEM((6, length * rows, 8, cells_z), f32),
            pltpu.VMEM((length * rows, 8, cells_z), f32),
            pltpu.VMEM(((length + 2) * rows, 8, cells_z), f32),
        ],
    )(source_x, source_y, source_z, station_x, station_y, station_z, full, cnt, total)

    keep = cells_y // cores
    summed, arrivals = pl.pallas_call(
        functools.partial(reduce_kernel, cores),
        name="reduce",
        out_shape=(
            jax.ShapeDtypeStruct((depth, keep, cells_z), f32),
            jax.ShapeDtypeStruct((2, 1, share), f32),
        ),
        in_specs=[VMEM, VMEM],
        out_specs=(VMEM, VMEM),
        scratch_shapes=[
            pltpu.VMEM((2 * cores, depth, keep, cells_z), f32),
            pltpu.SemaphoreType.DMA((2 * cores,)),
            pltpu.SemaphoreType.DMA((2 * cores,)),
            pltpu.SemaphoreType.DMA,
            pltpu.SemaphoreType.DMA,
        ],
        compiler_params=pltpu.CompilerParams(collective_id=1, has_side_effects=True),
    )(adj, arr)
    own = lax.dynamic_slice_in_dim(slowness, lax.axis_index("src") * keep, keep, axis=1)
    return own * summed, arrivals[:, 0]


def solution(mesh):
    in_specs = (P("brick", None, None), P("src"), P("src"), P("src"), P(), P(), P(), P("src", None))
    out_specs = (P("brick", "src", None), P("src", "brick"))
    return jax.shard_map(
        per_device, mesh=mesh, in_specs=in_specs, out_specs=out_specs, check_vma=False
    )
```

```python
import functools

import jax
import jax.numpy as jnp
from jax import lax
from jax.experimental import pallas as pl
from jax.experimental.pallas import tpu as pltpu
from jax.sharding import PartitionSpec as P

ITERS = 16

spacing = 0.015625
big_value = 1000000.0
start_slowness = 2.0
half_step = 0.5 * spacing
LOW = 4
FORWARD = 8
BACKWARD = 4

VMEM = pl.BlockSpec(memory_space=pltpu.VMEM)
SMEM = pl.BlockSpec(memory_space=pltpu.SMEM)
MESH = pl.DeviceIdType.MESH


def remote(src, dst, send_sem, recv_sem, core, brick):
    return pltpu.make_async_remote_copy(
        src_ref=src,
        dst_ref=dst,
        send_sem=send_sem,
        recv_sem=recv_sem,
        device_id={"src": core, "brick": brick},
        device_id_type=MESH,
    )


def window(pair_depth, grid_x, margin):
    length = min(grid_x, pair_depth + 2 * margin)
    pair = lax.axis_index("brick") // 2
    return jnp.clip(pair * pair_depth - margin, 0, grid_x - length), length


def stations(grid_x, cells_y, pair_depth, stx_ref, sty_ref, stz_ref, obs_ref, cnt_ref, sum_ref, table):
    rec = stx_ref.shape[1]
    cells_z = cnt_ref.shape[2]
    rows_y = cells_y // 8
    shift = rows_y.bit_length() - 1
    low, length = window(pair_depth, grid_x, ITERS)
    parity = lax.rem(lax.axis_index("brick"), 2)
    sty = sty_ref[...]
    row = (stx_ref[...] - low) * cells_y + (sty & (rows_y - 1)) * 8 + (sty >> shift)
    seen = obs_ref[pl.ds(parity, 1), :]
    hi = seen.astype(jnp.bfloat16).astype(jnp.float32)
    rest = seen - hi
    mid = rest.astype(jnp.bfloat16).astype(jnp.float32)
    lo = rest - mid
    hit = lax.broadcasted_iota(jnp.int32, (cells_z, rec), 0) == stz_ref[...]
    for part, value in enumerate((jnp.ones_like(seen), hi, mid, lo)):
        table[pl.ds(part * cells_z, cells_z), :] = jnp.where(hit, value, 0.0).astype(jnp.bfloat16)
    block = 256
    tiles = block // 8

    def tally(step):
        rows = lax.broadcasted_iota(jnp.int32, (block, rec), 0) + step * block
        pick = jnp.where(rows == row, 1.0, 0.0).astype(jnp.bfloat16)
        got = lax.dot_general(
            pick, table[...], (((1,), (1,)), ((), ())), preferred_element_type=jnp.float32
        )
        cnt_ref[pl.ds(step * tiles, tiles)] = got[:, :cells_z].reshape(tiles, 8, cells_z)
        total = got[:, cells_z : 2 * cells_z] + (
            got[:, 2 * cells_z : 3 * cells_z] + got[:, 3 * cells_z :]
        )
        sum_ref[pl.ds(step * tiles, tiles)] = total.reshape(tiles, 8, cells_z)

    return length * cells_y // block, tally


def gather_kernel(
    bricks,
    pair_depth,
    slow_ref,
    stx_ref,
    sty_ref,
    stz_ref,
    obs_ref,
    full_ref,
    cnt_ref,
    sum_ref,
    table,
    send_sem,
    recv_sem,
    twin_sem,
    own_sem,
):
    depth = slow_ref.shape[0]
    half = depth // 2
    lines = bricks // LOW
    me = lax.axis_index("brick")
    core = lax.axis_index("src")
    h = lax.rem(core, 2)
    twin = core + 1 - 2 * h
    line = me // LOW
    bit_x = lax.rem(me, 2)
    bit_y = lax.rem(me // 2, 2)
    flip_x = 1 - 2 * bit_x
    flip_y = 2 - 4 * bit_y
    first = me + flip_x * (1 - h) + flip_y * h
    second = me + flip_y * (1 - h) + flip_x * h
    corner = me + flip_x + flip_y
    has_down = line > 0
    has_up = line < lines - 1

    def piece(q, part):
        return full_ref.at[pl.ds(q * depth + part * half, half)]

    def copy(kind, q, brick, own=False):
        src = slow_ref.at[pl.ds(h * half, half)] if own else piece(q, h)
        return remote(src, piece(q, h), send_sem.at[kind, q], recv_sem.at[q], core, brick)

    def twin_copy(q):
        return remote(piece(q, h), piece(q, h), send_sem.at[4, q], twin_sem.at[q], twin, me)

    barrier = pltpu.get_barrier_semaphore()

    def greet(c, b):
        pl.semaphore_signal(barrier, inc=1, device_id={"src": c, "brick": b}, device_id_type=MESH)

    greet(twin, me)
    greet(core, first)
    greet(core, second)
    pl.when(has_down)(lambda: greet(core, me - LOW))
    pl.when(has_up)(lambda: greet(core, me + LOW))
    pl.semaphore_wait(barrier, 3 + has_down.astype(jnp.int32) + has_up.astype(jnp.int32))

    def sends(q, own, to_down, to_up, wait):
        def go(c):
            c.wait_send() if wait else c.start()

        if to_down is not None:
            pl.when(to_down)(lambda: go(copy(0, q, me - LOW, own)))
        if to_up is not None:
            pl.when(to_up)(lambda: go(copy(1, q, me + LOW, own)))
        go(copy(2, q, first, own))
        go(copy(3, q, second, own))

    own_copy = pltpu.make_async_copy(slow_ref, full_ref.at[pl.ds(me * depth, depth)], own_sem)
    sends(me, True, has_down, has_up, False)
    own_copy.start()

    def arrived(q):
        remote(piece(q, h), piece(q, h), send_sem.at[0, q], recv_sem.at[q], core, first).wait_recv()

    def on_line(base, i, act):
        pl.when((i < lines) & (line >= i))(lambda: act(base - LOW * i, -1))
        pl.when((i < lines) & (line + i < lines))(lambda: act(base + LOW * i, 1))

    def both(base, i, act):
        pl.when(i == 0)(lambda: act(base, 0))
        pl.when(i > 0)(lambda: on_line(base, i, act))

    def from_line(wait):
        def act(q, side):
            if not wait:
                arrived(q)
            sends(q, False, has_down if side > 0 else None, has_up if side < 0 else None, wait)
            c = twin_copy(q)
            c.wait_send() if wait else c.start()

        return act

    def from_first(wait):
        def act(q, side):
            if not wait:
                arrived(q)
            c = copy(3, q, second)
            c.wait_send() if wait else c.start()
            c = twin_copy(q)
            c.wait_send() if wait else c.start()

        return act

    def from_second(wait):
        def act(q, side):
            if not wait:
                arrived(q)
            c = twin_copy(q)
            c.wait_send() if wait else c.start()

        return act

    def turn(i, wait):
        on_line(me, i, from_line(wait))
        both(first, i - 1, from_first(wait))
        both(second, i - 1, from_second(wait))
        pl.when(i >= 2)(lambda: both(corner, i - 2, from_second(wait)))

    grid_x, cells_y, _ = full_ref.shape
    blocks, tally = stations(
        grid_x, cells_y, pair_depth, stx_ref, sty_ref, stz_ref, obs_ref, cnt_ref, sum_ref, table
    )
    share = -(-blocks // (lines + 1))

    @pl.loop(1, lines + 2)
    def _(i):
        turn(i, False)

        @pl.loop(0, share)
        def _(j):
            step = (i - 1) * share + j
            pl.when(step < blocks)(lambda: tally(step))

    own_copy.wait()
    sends(me, True, has_down, has_up, True)

    @pl.loop(1, lines + 2)
    def _(i):
        turn(i, True)

    @pl.loop(0, bricks)
    def _(q):
        @pl.when(q != me)
        def _():
            remote(piece(q, 1 - h), piece(q, 1 - h), send_sem.at[4, q], twin_sem.at[q], twin, me).wait_recv()


def solve_kernel(
    pair_depth,
    sx_ref,
    sy_ref,
    sz_ref,
    stx_ref,
    sty_ref,
    stz_ref,
    slow_ref,
    cnt_ref,
    sum_ref,
    adj_ref,
    arr_ref,
    time,
    cost,
    picked,
    weight,
    supply,
    field,
):
    grid_x, cells_y, cells_z = slow_ref.shape
    rows = cells_y // 8
    shift = rows.bit_length() - 1
    brick = lax.axis_index("brick")
    parity = lax.rem(brick, 2)
    pair = brick // 2
    lane = lax.broadcasted_iota(jnp.int32, (8, cells_z), 1)
    sub = lax.broadcasted_iota(jnp.int32, (8, cells_z), 0)
    lane_first = lane == 0
    lane_last = lane == cells_z - 1
    sub_first = sub == 0
    sub_last = sub == 7
    index_up = jnp.where(lane_last, cells_z - 2, lane + 1)
    index_down = jnp.where(lane_first, 1, lane - 1)

    def layer_of(ref, x):
        return tuple(ref[x * rows + v] for v in range(rows))

    def y_up(cur, v):
        return cur[v + 1] if v + 1 < rows else pltpu.roll(cur[0], 7, 0)

    def y_down(cur, v):
        return cur[v - 1] if v else pltpu.roll(cur[rows - 1], 1, 0)

    def z_up(one):
        return pltpu.roll(one, cells_z - 1, 1)

    def z_down(one):
        return pltpu.roll(one, 1, 1)

    sx = sx_ref[parity]
    sy = sy_ref[parity]
    sz = sz_ref[parity]
    dz = (lane - sz).astype(jnp.float32)
    flat = []
    for v in range(rows):
        dy = (sub * rows + v - sy).astype(jnp.float32)
        flat.append(dy * dy + dz * dz)

    @pl.loop(0, grid_x)
    def _(x):
        dx = (x - sx).astype(jnp.float32)
        for v in range(rows):
            slow = slow_ref[x, pl.ds(v, 8, stride=rows), :]
            start = (start_slowness * spacing) * jnp.sqrt(dx * dx + flat[v])
            cost[x * rows + v] = (2.0 * half_step) * slow
            time[(x + 1) * rows + v] = start + half_step * slow

    def pads(value):
        for v in range(rows):
            time[v] = jnp.full((8, cells_z), value, jnp.float32)
            time[(grid_x + 1) * rows + v] = jnp.full((8, cells_z), value, jnp.float32)

    pads(big_value)
    group = FORWARD

    def forward(x, prev, cur):
        nxt = layer_of(time, x + 2)
        for v in range(rows):
            one = cur[v]
            up = y_up(cur, v)
            down = y_down(cur, v)
            if v + 1 == rows:
                up = jnp.where(sub_last, big_value, up)
            if v == 0:
                down = jnp.where(sub_first, big_value, down)
            ahead = jnp.take_along_axis(one, index_up, axis=1)
            behind = jnp.take_along_axis(one, index_down, axis=1)
            low = jnp.minimum(
                jnp.minimum(jnp.minimum(prev[v], nxt[v]), jnp.minimum(up, down)), jnp.minimum(ahead, behind)
            )
            time[(x + 1) * rows + v] = jnp.minimum(one, low + cost[x * rows + v])
        return nxt

    @pl.loop(0, ITERS)
    def _(sweep):
        def body(i, carry):
            prev, cur = carry
            for j in range(group):
                nxt = forward(i * group + j, prev, cur)
                prev, cur = cur, nxt
            return prev, cur

        lax.fori_loop(0, grid_x // group, body, (layer_of(time, 0), layer_of(time, 1)))

    @pl.loop(0, grid_x)
    def _(x):
        for v in range(rows):
            time[(x + 1) * rows + v] = time[(x + 1) * rows + v] - 0.5 * cost[x * rows + v]

    pads(-big_value)

    count = picked.shape[0]
    line = lax.broadcasted_iota(jnp.int32, (1, cells_z), 1)
    unroll = 8

    @pl.loop(0, count // unroll)
    def _(i):
        for j in range(unroll):
            r = pair * count + i * unroll + j
            y = sty_ref[r]
            at = (stx_ref[r] + 1) * rows + (y & (rows - 1))
            got = time[at, pl.ds(y >> shift, 1), :]
            picked[pl.ds(i * unroll + j, 1), :] = jnp.where(line == stz_ref[r], got, 0.0)

    arrived = jnp.sum(jnp.transpose(picked[...]), axis=0, keepdims=True)
    arr_ref[0] = arrived[:, : count // 2]
    arr_ref[1] = arrived[:, count // 2 :]

    base, length = window(pair_depth, grid_x, ITERS - 1)
    outer, _ = window(pair_depth, grid_x, ITERS)

    def weigh(x, prev, cur):
        nxt = layer_of(time, x + 2)
        spot = (x - base) * rows
        for v in range(rows):
            one = cur[v]

            def gain(other):
                return jnp.maximum(other - one, 0.0)

            up = gain(y_up(cur, v))
            down = gain(y_down(cur, v))
            if v + 1 == rows:
                up = jnp.where(sub_last, 0.0, up)
            if v == 0:
                down = jnp.where(sub_first, 0.0, down)
            parts = (
                gain(prev[v]),
                gain(nxt[v]),
                down,
                up,
                jnp.where(lane_first, 0.0, gain(z_down(one))),
                jnp.where(lane_last, 0.0, gain(z_up(one))),
            )
            total = ((parts[0] + parts[1]) + (parts[2] + parts[3])) + (parts[4] + parts[5])
            inverse = 1.0 / (1.0 + total * (1.0 / spacing))
            scaled = inverse * (1.0 / spacing)
            for k, part in enumerate(parts):
                weight[k, spot + v] = part * scaled
            here = (x - outer) * rows + v
            value = (cnt_ref[here] * one - sum_ref[here]) * inverse
            supply[spot + v] = value
            field[spot + rows + v] = value
        return nxt

    def weigh_body(i, carry):
        prev, cur = carry
        for j in range(2):
            nxt = weigh(base + i * 2 + j, prev, cur)
            prev, cur = cur, nxt
        return prev, cur

    lax.fori_loop(0, length // 2, weigh_body, (layer_of(time, base), layer_of(time, base + 1)))
    for v in range(rows):
        field[v] = jnp.zeros((8, cells_z), jnp.float32)
        field[(length + 1) * rows + v] = jnp.zeros((8, cells_z), jnp.float32)

    def backward(x, prev, cur):
        nxt = layer_of(field, x + 2)
        for v in range(rows):
            one = cur[v]
            spot = x * rows + v
            acc = supply[spot] + weight[0, spot] * prev[v]
            acc = acc + weight[1, spot] * nxt[v]
            side = weight[2, spot] * y_down(cur, v) + weight[3, spot] * y_up(cur, v)
            acc = acc + side
            acc = acc + (weight[4, spot] * z_down(one) + weight[5, spot] * z_up(one))
            field[spot + rows] = acc
        return nxt

    @pl.loop(2, ITERS + 1)
    def _(sweep):
        margin = ITERS - sweep
        span = jnp.minimum(grid_x, (pair_depth + 2 * margin + BACKWARD - 1) // BACKWARD * BACKWARD)
        first = jnp.clip(pair * pair_depth - margin, 0, grid_x - span) - base

        def body(i, carry):
            prev, cur = carry
            for j in range(BACKWARD):
                nxt = backward(first + i * BACKWARD + j, prev, cur)
                prev, cur = cur, nxt
            return prev, cur

        lax.fori_loop(0, span // BACKWARD, body, (layer_of(field, first), layer_of(field, first + 1)))

    mine = pair * pair_depth - base + 1
    for x in range(pair_depth):
        for v in range(rows):
            adj_ref[x, pl.ds(v, 8, stride=rows), :] = field[(mine + x) * rows + v]


def reduce_kernel(cores, adj_ref, arr_ref, out_ref, got_ref, slots, send_sem, recv_sem, word_send, word_recv):
    depth, keep, _ = out_ref.shape
    brick = lax.axis_index("brick")
    core = lax.axis_index("src")
    parity = lax.rem(brick, 2)
    other = brick + 1 - 2 * parity
    me = core * 2 + parity

    def target(k):
        c = lax.rem(core + k // 2, cores)
        p = lax.rem(parity + k % 2, 2)
        return c, p, brick - parity + p

    def copy(k):
        c, p, b = target(k)
        return remote(
            adj_ref.at[pl.ds(p * depth, depth), pl.ds(c * keep, keep)],
            slots.at[k],
            send_sem.at[k],
            recv_sem.at[k],
            c,
            b,
        )

    barrier = pltpu.get_barrier_semaphore()
    for k in range(1, 2 * cores):
        c, _, b = target(k)
        pl.semaphore_signal(barrier, inc=1, device_id={"src": c, "brick": b}, device_id_type=MESH)
    pl.semaphore_wait(barrier, 2 * cores - 1)
    word = remote(arr_ref.at[1 - parity], got_ref.at[parity], word_send, word_recv, core, other)
    word.start()
    for k in range(1, 2 * cores):
        copy(k).start()
    got_ref[parity] = arr_ref[parity]
    total = adj_ref[pl.ds(parity * depth, depth), pl.ds(pl.multiple_of(core * keep, 8), keep), :]
    for k in range(1, 2 * cores):
        copy(k).wait_recv()
        total = total + slots[k]
    out_ref[...] = total
    for k in range(1, 2 * cores):
        copy(k).wait_send()
    word.wait_send()
    remote(arr_ref.at[parity], got_ref.at[1 - parity], word_send, word_recv, core, other).wait_recv()


def per_device(slowness, source_x, source_y, source_z, station_x, station_y, station_z, observed):
    bricks = lax.axis_size("brick")
    cores = lax.axis_size("src")
    depth, cells_y, cells_z = slowness.shape
    grid_x = depth * bricks
    rec = station_x.shape[0]
    pair_depth = 2 * depth
    rows = cells_y // 8
    assert source_x.shape[0] == 2 and bricks % LOW == 0 and cores % 2 == 0
    f32 = jnp.float32

    wide = min(grid_x, pair_depth + 2 * ITERS)
    field = jax.ShapeDtypeStruct((wide * rows, 8, cells_z), f32)
    full, cnt, total = pl.pallas_call(
        functools.partial(gather_kernel, bricks, pair_depth),
        name="gather",
        out_shape=(jax.ShapeDtypeStruct((grid_x, cells_y, cells_z), f32), field, field),
        in_specs=[VMEM] * 5,
        out_specs=(VMEM, VMEM, VMEM),
        scratch_shapes=[
            pltpu.VMEM((4 * cells_z, rec), jnp.bfloat16),
            pltpu.SemaphoreType.DMA((5, bricks)),
            pltpu.SemaphoreType.DMA((bricks,)),
            pltpu.SemaphoreType.DMA((bricks,)),
            pltpu.SemaphoreType.DMA,
        ],
        compiler_params=pltpu.CompilerParams(collective_id=0, has_side_effects=True),
    )(slowness, station_x[None], station_y[None], station_z[None], observed)

    length = min(grid_x, pair_depth + 2 * (ITERS - 1))
    share = rec // bricks
    adj, arr = pl.pallas_call(
        functools.partial(solve_kernel, pair_depth),
        name="solve",
        out_shape=(
            jax.ShapeDtypeStruct((pair_depth, cells_y, cells_z), f32),
            jax.ShapeDtypeStruct((2, 1, share), f32),
        ),
        in_specs=[SMEM] * 6 + [VMEM] * 3,
        out_specs=(VMEM, VMEM),
        scratch_shapes=[
            pltpu.VMEM(((grid_x + 2) * rows, 8, cells_z), f32),
            pltpu.VMEM((grid_x * rows, 8, cells_z), f32),
            pltpu.VMEM((2 * share, cells_z), f32),
            pltpu.VMEM((6, length * rows, 8, cells_z), f32),
            pltpu.VMEM((length * rows, 8, cells_z), f32),
            pltpu.VMEM(((length + 2) * rows, 8, cells_z), f32),
        ],
    )(source_x, source_y, source_z, station_x, station_y, station_z, full, cnt, total)

    keep = cells_y // cores
    summed, arrivals = pl.pallas_call(
        functools.partial(reduce_kernel, cores),
        name="reduce",
        out_shape=(
            jax.ShapeDtypeStruct((depth, keep, cells_z), f32),
            jax.ShapeDtypeStruct((2, 1, share), f32),
        ),
        in_specs=[VMEM, VMEM],
        out_specs=(VMEM, VMEM),
        scratch_shapes=[
            pltpu.VMEM((2 * cores, depth, keep, cells_z), f32),
            pltpu.SemaphoreType.DMA((2 * cores,)),
            pltpu.SemaphoreType.DMA((2 * cores,)),
            pltpu.SemaphoreType.DMA,
            pltpu.SemaphoreType.DMA,
        ],
        compiler_params=pltpu.CompilerParams(collective_id=1, has_side_effects=True),
    )(adj, arr)
    own = lax.dynamic_slice_in_dim(slowness, lax.axis_index("src") * keep, keep, axis=1)
    return own * summed, arrivals[:, 0]


def solution(mesh):
    in_specs = (P("brick", None, None), P("src"), P("src"), P("src"), P(), P(), P(), P("src", None))
    out_specs = (P("brick", "src", None), P("src", "brick"))
    return jax.shard_map(
        per_device, mesh=mesh, in_specs=in_specs, out_specs=out_specs, check_vma=False
    )
```

```python
import functools

import jax
import jax.numpy as jnp
from jax import lax
from jax.experimental import pallas as pl
from jax.experimental.pallas import tpu as pltpu
from jax.sharding import PartitionSpec as P

ITERS = 16

spacing = 0.015625
big_value = 1000000.0
start_slowness = 2.0
half_step = 0.5 * spacing
LOW = 4
FORWARD = 8
BACKWARD = 4

VMEM = pl.BlockSpec(memory_space=pltpu.VMEM)
SMEM = pl.BlockSpec(memory_space=pltpu.SMEM)
MESH = pl.DeviceIdType.MESH


def remote(src, dst, send_sem, recv_sem, core, brick):
    return pltpu.make_async_remote_copy(
        src_ref=src,
        dst_ref=dst,
        send_sem=send_sem,
        recv_sem=recv_sem,
        device_id={"src": core, "brick": brick},
        device_id_type=MESH,
    )


def window(pair_depth, grid_x, margin):
    length = min(grid_x, pair_depth + 2 * margin)
    pair = lax.axis_index("brick") // 2
    return jnp.clip(pair * pair_depth - margin, 0, grid_x - length), length


def stations(grid_x, cells_y, pair_depth, stx_ref, sty_ref, stz_ref, obs_ref, cnt_ref, sum_ref, table):
    rec = stx_ref.shape[1]
    cells_z = cnt_ref.shape[2]
    rows_y = cells_y // 8
    shift = rows_y.bit_length() - 1
    low, length = window(pair_depth, grid_x, ITERS)
    parity = lax.rem(lax.axis_index("brick"), 2)
    sty = sty_ref[...]
    row = (stx_ref[...] - low) * cells_y + (sty & (rows_y - 1)) * 8 + (sty >> shift)
    seen = obs_ref[pl.ds(parity, 1), :]
    hi = seen.astype(jnp.bfloat16).astype(jnp.float32)
    rest = seen - hi
    mid = rest.astype(jnp.bfloat16).astype(jnp.float32)
    lo = rest - mid
    hit = lax.broadcasted_iota(jnp.int32, (cells_z, rec), 0) == stz_ref[...]
    for part, value in enumerate((jnp.ones_like(seen), hi, mid, lo)):
        table[pl.ds(part * cells_z, cells_z), :] = jnp.where(hit, value, 0.0).astype(jnp.bfloat16)
    block = 256
    tiles = block // 8

    def tally(step):
        rows = lax.broadcasted_iota(jnp.int32, (block, rec), 0) + step * block
        pick = jnp.where(rows == row, 1.0, 0.0).astype(jnp.bfloat16)
        got = lax.dot_general(
            pick, table[...], (((1,), (1,)), ((), ())), preferred_element_type=jnp.float32
        )
        cnt_ref[pl.ds(step * tiles, tiles)] = got[:, :cells_z].reshape(tiles, 8, cells_z)
        total = got[:, cells_z : 2 * cells_z] + (
            got[:, 2 * cells_z : 3 * cells_z] + got[:, 3 * cells_z :]
        )
        sum_ref[pl.ds(step * tiles, tiles)] = total.reshape(tiles, 8, cells_z)

    return length * cells_y // block, tally


def gather_kernel(
    bricks,
    pair_depth,
    slow_ref,
    stx_ref,
    sty_ref,
    stz_ref,
    obs_ref,
    full_ref,
    cnt_ref,
    sum_ref,
    table,
    line_sem,
    send_sem,
    recv_sem,
    twin_sem,
    own_sem,
):
    depth = slow_ref.shape[0]
    half = depth // 2
    lines = bricks // LOW
    me = lax.axis_index("brick")
    core = lax.axis_index("src")
    h = lax.rem(core, 2)
    twin = core + 1 - 2 * h
    line = me // LOW
    bit_x = lax.rem(me, 2)
    bit_y = lax.rem(me // 2, 2)
    flip_x = 1 - 2 * bit_x
    flip_y = 2 - 4 * bit_y
    first = me + flip_x * (1 - h) + flip_y * h
    second = me + flip_y * (1 - h) + flip_x * h
    corner = me + flip_x + flip_y

    def piece(q, part):
        return full_ref.at[pl.ds(q * depth + part * half, half)]

    def copy(kind, q, brick, own=False):
        src = slow_ref.at[pl.ds(h * half, half)] if own else piece(q, h)
        return remote(src, piece(q, h), send_sem.at[kind, q], recv_sem.at[q], core, brick)

    def twin_copy(q):
        return remote(piece(q, h), piece(q, h), send_sem.at[2, q], twin_sem.at[q], twin, me)

    barrier = pltpu.get_barrier_semaphore()

    def greet(c, b):
        pl.semaphore_signal(barrier, inc=1, device_id={"src": c, "brick": b}, device_id_type=MESH)

    greet(twin, me)
    greet(core, first)
    greet(core, second)
    for k in range(1, lines):
        pl.when(line >= k)(lambda k=k: greet(core, me - LOW * k))
        pl.when(line + k < lines)(lambda k=k: greet(core, me + LOW * k))
    pl.semaphore_wait(barrier, lines + 2)

    def along(k, up):
        dst = piece(me, h)
        src = slow_ref.at[pl.ds(h * half, half)]
        brick = me + LOW * k if up else me - LOW * k
        return remote(src, dst, line_sem.at[int(up), k], recv_sem.at[me], core, brick)

    def own_line(k, wait):
        def go(up):
            c = along(k, up)
            c.wait_send() if wait else c.start()

        pl.when(line >= k)(lambda: go(False))
        pl.when(line + k < lines)(lambda: go(True))

    def sends(q, own, wait):
        for kind, brick in ((0, first), (1, second)):
            c = copy(kind, q, brick, own)
            c.wait_send() if wait else c.start()

    own_copy = pltpu.make_async_copy(slow_ref, full_ref.at[pl.ds(me * depth, depth)], own_sem)
    for k in range(1, lines):
        own_line(k, False)
        if k == 1:
            sends(me, True, False)
    own_copy.start()

    def arrived(q):
        remote(piece(q, h), piece(q, h), send_sem.at[0, q], recv_sem.at[q], core, first).wait_recv()

    def on_line(base, i, act):
        pl.when((i < lines) & (line >= i))(lambda: act(base - LOW * i, -1))
        pl.when((i < lines) & (line + i < lines))(lambda: act(base + LOW * i, 1))

    def both(base, i, act):
        pl.when(i == 0)(lambda: act(base, 0))
        pl.when(i > 0)(lambda: on_line(base, i, act))

    def from_line(wait):
        def act(q, side):
            if not wait:
                arrived(q)
            sends(q, False, wait)
            c = twin_copy(q)
            c.wait_send() if wait else c.start()

        return act

    def from_first(wait):
        def act(q, side):
            if not wait:
                arrived(q)
            c = copy(1, q, second)
            c.wait_send() if wait else c.start()
            c = twin_copy(q)
            c.wait_send() if wait else c.start()

        return act

    def from_second(wait):
        def act(q, side):
            if not wait:
                arrived(q)
            c = twin_copy(q)
            c.wait_send() if wait else c.start()

        return act

    def turn(i, wait):
        on_line(me, i, from_line(wait))
        both(first, i - 1, from_first(wait))
        both(second, i - 1, from_second(wait))
        pl.when(i >= 2)(lambda: both(corner, i - 2, from_second(wait)))

    grid_x, cells_y, _ = full_ref.shape
    blocks, tally = stations(
        grid_x, cells_y, pair_depth, stx_ref, sty_ref, stz_ref, obs_ref, cnt_ref, sum_ref, table
    )
    share = -(-blocks // (lines + 1))

    @pl.loop(1, lines + 2)
    def _(i):
        turn(i, False)

        @pl.loop(0, share)
        def _(j):
            step = (i - 1) * share + j
            pl.when(step < blocks)(lambda: tally(step))

    own_copy.wait()
    sends(me, True, True)
    for k in range(1, lines):
        own_line(k, True)

    @pl.loop(1, lines + 2)
    def _(i):
        turn(i, True)

    @pl.loop(0, bricks)
    def _(q):
        @pl.when(q != me)
        def _():
            remote(piece(q, 1 - h), piece(q, 1 - h), send_sem.at[2, q], twin_sem.at[q], twin, me).wait_recv()


def solve_kernel(
    pair_depth,
    sx_ref,
    sy_ref,
    sz_ref,
    stx_ref,
    sty_ref,
    stz_ref,
    slow_ref,
    cnt_ref,
    sum_ref,
    adj_ref,
    arr_ref,
    time,
    cost,
    picked,
    weight,
    supply,
    field,
):
    grid_x, cells_y, cells_z = slow_ref.shape
    rows = cells_y // 8
    shift = rows.bit_length() - 1
    brick = lax.axis_index("brick")
    parity = lax.rem(brick, 2)
    pair = brick // 2
    lane = lax.broadcasted_iota(jnp.int32, (8, cells_z), 1)
    sub = lax.broadcasted_iota(jnp.int32, (8, cells_z), 0)
    lane_first = lane == 0
    lane_last = lane == cells_z - 1
    sub_first = sub == 0
    sub_last = sub == 7
    index_up = jnp.where(lane_last, cells_z - 2, lane + 1)
    index_down = jnp.where(lane_first, 1, lane - 1)

    def layer_of(ref, x):
        return tuple(ref[x * rows + v] for v in range(rows))

    def y_up(cur, v):
        return cur[v + 1] if v + 1 < rows else pltpu.roll(cur[0], 7, 0)

    def y_down(cur, v):
        return cur[v - 1] if v else pltpu.roll(cur[rows - 1], 1, 0)

    def z_up(one):
        return jnp.take_along_axis(one, index_up, axis=1)

    def z_down(one):
        return jnp.take_along_axis(one, index_down, axis=1)

    sx = sx_ref[parity]
    sy = sy_ref[parity]
    sz = sz_ref[parity]
    dz = (lane - sz).astype(jnp.float32)
    flat = []
    for v in range(rows):
        dy = (sub * rows + v - sy).astype(jnp.float32)
        flat.append(dy * dy + dz * dz)

    @pl.loop(0, grid_x)
    def _(x):
        dx = (x - sx).astype(jnp.float32)
        for v in range(rows):
            slow = slow_ref[x, pl.ds(v, 8, stride=rows), :]
            start = (start_slowness * spacing) * jnp.sqrt(dx * dx + flat[v])
            cost[x * rows + v] = (2.0 * half_step) * slow
            time[(x + 1) * rows + v] = start + half_step * slow

    def pads(value):
        for v in range(rows):
            time[v] = jnp.full((8, cells_z), value, jnp.float32)
            time[(grid_x + 1) * rows + v] = jnp.full((8, cells_z), value, jnp.float32)

    pads(big_value)
    group = FORWARD

    def forward(x, prev, cur):
        nxt = layer_of(time, x + 2)
        for v in range(rows):
            one = cur[v]
            up = y_up(cur, v)
            down = y_down(cur, v)
            if v + 1 == rows:
                up = jnp.where(sub_last, big_value, up)
            if v == 0:
                down = jnp.where(sub_first, big_value, down)
            ahead = z_up(one)
            behind = z_down(one)
            low = jnp.minimum(
                jnp.minimum(jnp.minimum(prev[v], nxt[v]), jnp.minimum(up, down)), jnp.minimum(ahead, behind)
            )
            time[(x + 1) * rows + v] = jnp.minimum(one, low + cost[x * rows + v])
        return nxt

    @pl.loop(0, ITERS)
    def _(sweep):
        def body(i, carry):
            prev, cur = carry
            for j in range(group):
                nxt = forward(i * group + j, prev, cur)
                prev, cur = cur, nxt
            return prev, cur

        lax.fori_loop(0, grid_x // group, body, (layer_of(time, 0), layer_of(time, 1)))

    @pl.loop(0, grid_x)
    def _(x):
        for v in range(rows):
            time[(x + 1) * rows + v] = time[(x + 1) * rows + v] - 0.5 * cost[x * rows + v]

    pads(-big_value)

    count = picked.shape[0]
    line = lax.broadcasted_iota(jnp.int32, (1, cells_z), 1)
    unroll = 8

    @pl.loop(0, count // unroll)
    def _(i):
        for j in range(unroll):
            r = pair * count + i * unroll + j
            y = sty_ref[r]
            at = (stx_ref[r] + 1) * rows + (y & (rows - 1))
            got = time[at, pl.ds(y >> shift, 1), :]
            picked[pl.ds(i * unroll + j, 1), :] = jnp.where(line == stz_ref[r], got, 0.0)

    arrived = jnp.sum(jnp.transpose(picked[...]), axis=0, keepdims=True)
    arr_ref[0] = arrived[:, : count // 2]
    arr_ref[1] = arrived[:, count // 2 :]

    base, length = window(pair_depth, grid_x, ITERS - 1)
    outer, _ = window(pair_depth, grid_x, ITERS)

    def weigh(x, prev, cur):
        nxt = layer_of(time, x + 2)
        spot = (x - base) * rows
        for v in range(rows):
            one = cur[v]

            def gain(other):
                return jnp.maximum(other - one, 0.0)

            up = gain(y_up(cur, v))
            down = gain(y_down(cur, v))
            if v + 1 == rows:
                up = jnp.where(sub_last, 0.0, up)
            if v == 0:
                down = jnp.where(sub_first, 0.0, down)
            parts = (
                gain(prev[v]),
                gain(nxt[v]),
                down,
                up,
                jnp.where(lane_first, 0.0, gain(z_down(one))),
                jnp.where(lane_last, 0.0, gain(z_up(one))),
            )
            total = ((parts[0] + parts[1]) + (parts[2] + parts[3])) + (parts[4] + parts[5])
            inverse = 1.0 / (1.0 + total * (1.0 / spacing))
            scaled = inverse * (1.0 / spacing)
            for k, part in enumerate(parts):
                weight[k, spot + v] = part * scaled
            here = (x - outer) * rows + v
            value = (cnt_ref[here] * one - sum_ref[here]) * inverse
            supply[spot + v] = value
            field[spot + rows + v] = value
        return nxt

    def weigh_body(i, carry):
        prev, cur = carry
        for j in range(2):
            nxt = weigh(base + i * 2 + j, prev, cur)
            prev, cur = cur, nxt
        return prev, cur

    lax.fori_loop(0, length // 2, weigh_body, (layer_of(time, base), layer_of(time, base + 1)))
    for v in range(rows):
        field[v] = jnp.zeros((8, cells_z), jnp.float32)
        field[(length + 1) * rows + v] = jnp.zeros((8, cells_z), jnp.float32)

    def backward(x, prev, cur):
        nxt = layer_of(field, x + 2)
        for v in range(rows):
            one = cur[v]
            spot = x * rows + v
            acc = supply[spot] + weight[0, spot] * prev[v]
            acc = acc + weight[1, spot] * nxt[v]
            side = weight[2, spot] * y_down(cur, v) + weight[3, spot] * y_up(cur, v)
            acc = acc + side
            acc = acc + (weight[4, spot] * z_down(one) + weight[5, spot] * z_up(one))
            field[spot + rows] = acc
        return nxt

    @pl.loop(2, ITERS + 1)
    def _(sweep):
        margin = ITERS - sweep
        span = jnp.minimum(grid_x, (pair_depth + 2 * margin + BACKWARD - 1) // BACKWARD * BACKWARD)
        first = jnp.clip(pair * pair_depth - margin, 0, grid_x - span) - base

        def body(i, carry):
            prev, cur = carry
            for j in range(BACKWARD):
                nxt = backward(first + i * BACKWARD + j, prev, cur)
                prev, cur = cur, nxt
            return prev, cur

        lax.fori_loop(0, span // BACKWARD, body, (layer_of(field, first), layer_of(field, first + 1)))

    mine = pair * pair_depth - base + 1
    for x in range(pair_depth):
        for v in range(rows):
            adj_ref[x, pl.ds(v, 8, stride=rows), :] = field[(mine + x) * rows + v]


def reduce_kernel(cores, adj_ref, arr_ref, out_ref, got_ref, slots, send_sem, recv_sem, word_send, word_recv):
    depth, keep, _ = out_ref.shape
    brick = lax.axis_index("brick")
    core = lax.axis_index("src")
    parity = lax.rem(brick, 2)
    other = brick + 1 - 2 * parity
    me = core * 2 + parity

    def target(k):
        c = lax.rem(core + k // 2, cores)
        p = lax.rem(parity + k % 2, 2)
        return c, p, brick - parity + p

    def copy(k):
        c, p, b = target(k)
        return remote(
            adj_ref.at[pl.ds(p * depth, depth), pl.ds(c * keep, keep)],
            slots.at[k],
            send_sem.at[k],
            recv_sem.at[k],
            c,
            b,
        )

    barrier = pltpu.get_barrier_semaphore()
    for k in range(1, 2 * cores):
        c, _, b = target(k)
        pl.semaphore_signal(barrier, inc=1, device_id={"src": c, "brick": b}, device_id_type=MESH)
    pl.semaphore_wait(barrier, 2 * cores - 1)
    word = remote(arr_ref.at[1 - parity], got_ref.at[parity], word_send, word_recv, core, other)
    word.start()
    for k in range(1, 2 * cores):
        copy(k).start()
    got_ref[parity] = arr_ref[parity]
    total = adj_ref[pl.ds(parity * depth, depth), pl.ds(pl.multiple_of(core * keep, 8), keep), :]
    for k in range(1, 2 * cores):
        copy(k).wait_recv()
        total = total + slots[k]
    out_ref[...] = total
    for k in range(1, 2 * cores):
        copy(k).wait_send()
    word.wait_send()
    remote(arr_ref.at[parity], got_ref.at[1 - parity], word_send, word_recv, core, other).wait_recv()


def per_device(slowness, source_x, source_y, source_z, station_x, station_y, station_z, observed):
    bricks = lax.axis_size("brick")
    cores = lax.axis_size("src")
    depth, cells_y, cells_z = slowness.shape
    grid_x = depth * bricks
    rec = station_x.shape[0]
    pair_depth = 2 * depth
    rows = cells_y // 8
    assert source_x.shape[0] == 2 and bricks % LOW == 0 and cores % 2 == 0
    f32 = jnp.float32

    wide = min(grid_x, pair_depth + 2 * ITERS)
    field = jax.ShapeDtypeStruct((wide * rows, 8, cells_z), f32)
    full, cnt, total = pl.pallas_call(
        functools.partial(gather_kernel, bricks, pair_depth),
        name="gather",
        out_shape=(jax.ShapeDtypeStruct((grid_x, cells_y, cells_z), f32), field, field),
        in_specs=[VMEM] * 5,
        out_specs=(VMEM, VMEM, VMEM),
        scratch_shapes=[
            pltpu.VMEM((4 * cells_z, rec), jnp.bfloat16),
            pltpu.SemaphoreType.DMA((2, bricks // LOW)),
            pltpu.SemaphoreType.DMA((3, bricks)),
            pltpu.SemaphoreType.DMA((bricks,)),
            pltpu.SemaphoreType.DMA((bricks,)),
            pltpu.SemaphoreType.DMA,
        ],
        compiler_params=pltpu.CompilerParams(collective_id=0, has_side_effects=True),
    )(slowness, station_x[None], station_y[None], station_z[None], observed)

    length = min(grid_x, pair_depth + 2 * (ITERS - 1))
    share = rec // bricks
    adj, arr = pl.pallas_call(
        functools.partial(solve_kernel, pair_depth),
        name="solve",
        out_shape=(
            jax.ShapeDtypeStruct((pair_depth, cells_y, cells_z), f32),
            jax.ShapeDtypeStruct((2, 1, share), f32),
        ),
        in_specs=[SMEM] * 6 + [VMEM] * 3,
        out_specs=(VMEM, VMEM),
        scratch_shapes=[
            pltpu.VMEM(((grid_x + 2) * rows, 8, cells_z), f32),
            pltpu.VMEM((grid_x * rows, 8, cells_z), f32),
            pltpu.VMEM((2 * share, cells_z), f32),
            pltpu.VMEM((6, length * rows, 8, cells_z), f32),
            pltpu.VMEM((length * rows, 8, cells_z), f32),
            pltpu.VMEM(((length + 2) * rows, 8, cells_z), f32),
        ],
    )(source_x, source_y, source_z, station_x, station_y, station_z, full, cnt, total)

    keep = cells_y // cores
    summed, arrivals = pl.pallas_call(
        functools.partial(reduce_kernel, cores),
        name="reduce",
        out_shape=(
            jax.ShapeDtypeStruct((depth, keep, cells_z), f32),
            jax.ShapeDtypeStruct((2, 1, share), f32),
        ),
        in_specs=[VMEM, VMEM],
        out_specs=(VMEM, VMEM),
        scratch_shapes=[
            pltpu.VMEM((2 * cores, depth, keep, cells_z), f32),
            pltpu.SemaphoreType.DMA((2 * cores,)),
            pltpu.SemaphoreType.DMA((2 * cores,)),
            pltpu.SemaphoreType.DMA,
            pltpu.SemaphoreType.DMA,
        ],
        compiler_params=pltpu.CompilerParams(collective_id=1, has_side_effects=True),
    )(adj, arr)
    own = lax.dynamic_slice_in_dim(slowness, lax.axis_index("src") * keep, keep, axis=1)
    return own * summed, arrivals[:, 0]


def solution(mesh):
    in_specs = (P("brick", None, None), P("src"), P("src"), P("src"), P(), P(), P(), P("src", None))
    out_specs = (P("brick", "src", None), P("src", "brick"))
    return jax.shard_map(
        per_device, mesh=mesh, in_specs=in_specs, out_specs=out_specs, check_vma=False
    )
```

```python
import functools

import jax
import jax.numpy as jnp
from jax import lax
from jax.experimental import pallas as pl
from jax.experimental.pallas import tpu as pltpu
from jax.sharding import PartitionSpec as P

ITERS = 16

spacing = 0.015625
big_value = 1000000.0
start_slowness = 2.0
half_step = 0.5 * spacing
LOW = 4
FORWARD = 8
BACKWARD = 4

VMEM = pl.BlockSpec(memory_space=pltpu.VMEM)
SMEM = pl.BlockSpec(memory_space=pltpu.SMEM)
MESH = pl.DeviceIdType.MESH


def remote(src, dst, send_sem, recv_sem, core, brick):
    return pltpu.make_async_remote_copy(
        src_ref=src,
        dst_ref=dst,
        send_sem=send_sem,
        recv_sem=recv_sem,
        device_id={"src": core, "brick": brick},
        device_id_type=MESH,
    )


def window(pair_depth, grid_x, margin):
    length = min(grid_x, pair_depth + 2 * margin)
    pair = lax.axis_index("brick") // 2
    return jnp.clip(pair * pair_depth - margin, 0, grid_x - length), length


def stations(grid_x, cells_y, pair_depth, stx_ref, sty_ref, stz_ref, obs_ref, cnt_ref, sum_ref, table):
    rec = stx_ref.shape[1]
    cells_z = cnt_ref.shape[2]
    rows_y = cells_y // 8
    shift = rows_y.bit_length() - 1
    low, length = window(pair_depth, grid_x, ITERS)
    parity = lax.rem(lax.axis_index("brick"), 2)
    sty = sty_ref[...]
    row = (stx_ref[...] - low) * cells_y + (sty & (rows_y - 1)) * 8 + (sty >> shift)
    seen = obs_ref[pl.ds(parity, 1), :]
    hi = seen.astype(jnp.bfloat16).astype(jnp.float32)
    rest = seen - hi
    mid = rest.astype(jnp.bfloat16).astype(jnp.float32)
    lo = rest - mid
    stz = stz_ref[...]
    hit = lax.broadcasted_iota(jnp.int32, (cells_z, rec), 0) == (stz & 1) * (cells_z // 2) + (stz >> 1)
    for part, value in enumerate((jnp.ones_like(seen), hi, mid, lo)):
        table[pl.ds(part * cells_z, cells_z), :] = jnp.where(hit, value, 0.0).astype(jnp.bfloat16)
    block = 256
    tiles = block // 8

    def tally(step):
        rows = lax.broadcasted_iota(jnp.int32, (block, rec), 0) + step * block
        pick = jnp.where(rows == row, 1.0, 0.0).astype(jnp.bfloat16)
        got = lax.dot_general(
            pick, table[...], (((1,), (1,)), ((), ())), preferred_element_type=jnp.float32
        )
        cnt_ref[pl.ds(step * tiles, tiles)] = got[:, :cells_z].reshape(tiles, 8, cells_z)
        total = got[:, cells_z : 2 * cells_z] + (
            got[:, 2 * cells_z : 3 * cells_z] + got[:, 3 * cells_z :]
        )
        sum_ref[pl.ds(step * tiles, tiles)] = total.reshape(tiles, 8, cells_z)

    return length * cells_y // block, tally


def gather_kernel(
    bricks,
    pair_depth,
    slow_ref,
    stx_ref,
    sty_ref,
    stz_ref,
    obs_ref,
    full_ref,
    cnt_ref,
    sum_ref,
    table,
    line_sem,
    send_sem,
    recv_sem,
    twin_sem,
    own_sem,
):
    depth = slow_ref.shape[0]
    half = depth // 2
    lines = bricks // LOW
    me = lax.axis_index("brick")
    core = lax.axis_index("src")
    h = lax.rem(core, 2)
    twin = core + 1 - 2 * h
    line = me // LOW
    bit_x = lax.rem(me, 2)
    bit_y = lax.rem(me // 2, 2)
    flip_x = 1 - 2 * bit_x
    flip_y = 2 - 4 * bit_y
    first = me + flip_x * (1 - h) + flip_y * h
    second = me + flip_y * (1 - h) + flip_x * h
    corner = me + flip_x + flip_y

    def piece(q, part):
        return full_ref.at[pl.ds(q * depth + part * half, half)]

    def copy(kind, q, brick, own=False):
        src = slow_ref.at[pl.ds(h * half, half)] if own else piece(q, h)
        return remote(src, piece(q, h), send_sem.at[kind, q], recv_sem.at[q], core, brick)

    def twin_copy(q):
        return remote(piece(q, h), piece(q, h), send_sem.at[2, q], twin_sem.at[q], twin, me)

    barrier = pltpu.get_barrier_semaphore()

    def greet(c, b):
        pl.semaphore_signal(barrier, inc=1, device_id={"src": c, "brick": b}, device_id_type=MESH)

    greet(twin, me)
    greet(core, first)
    greet(core, second)
    for k in range(1, lines):
        pl.when(line >= k)(lambda k=k: greet(core, me - LOW * k))
        pl.when(line + k < lines)(lambda k=k: greet(core, me + LOW * k))
    pl.semaphore_wait(barrier, lines + 2)

    def along(k, up):
        dst = piece(me, h)
        src = slow_ref.at[pl.ds(h * half, half)]
        brick = me + LOW * k if up else me - LOW * k
        return remote(src, dst, line_sem.at[int(up), k], recv_sem.at[me], core, brick)

    def own_line(k, wait):
        def go(up):
            c = along(k, up)
            c.wait_send() if wait else c.start()

        pl.when(line >= k)(lambda: go(False))
        pl.when(line + k < lines)(lambda: go(True))

    def sends(q, own, wait):
        for kind, brick in ((0, first), (1, second)):
            c = copy(kind, q, brick, own)
            c.wait_send() if wait else c.start()

    own_copy = pltpu.make_async_copy(slow_ref, full_ref.at[pl.ds(me * depth, depth)], own_sem)
    for k in range(1, lines):
        own_line(k, False)
        if k == 1:
            sends(me, True, False)
    own_copy.start()

    def arrived(q):
        remote(piece(q, h), piece(q, h), send_sem.at[0, q], recv_sem.at[q], core, first).wait_recv()

    def on_line(base, i, act):
        pl.when((i < lines) & (line >= i))(lambda: act(base - LOW * i, -1))
        pl.when((i < lines) & (line + i < lines))(lambda: act(base + LOW * i, 1))

    def both(base, i, act):
        pl.when(i == 0)(lambda: act(base, 0))
        pl.when(i > 0)(lambda: on_line(base, i, act))

    def from_line(wait):
        def act(q, side):
            if not wait:
                arrived(q)
            sends(q, False, wait)
            c = twin_copy(q)
            c.wait_send() if wait else c.start()

        return act

    def from_first(wait):
        def act(q, side):
            if not wait:
                arrived(q)
            c = copy(1, q, second)
            c.wait_send() if wait else c.start()
            c = twin_copy(q)
            c.wait_send() if wait else c.start()

        return act

    def from_second(wait):
        def act(q, side):
            if not wait:
                arrived(q)
            c = twin_copy(q)
            c.wait_send() if wait else c.start()

        return act

    def turn(i, wait):
        on_line(me, i, from_line(wait))
        both(first, i - 1, from_first(wait))
        both(second, i - 1, from_second(wait))
        pl.when(i >= 2)(lambda: both(corner, i - 2, from_second(wait)))

    grid_x, cells_y, _ = full_ref.shape
    blocks, tally = stations(
        grid_x, cells_y, pair_depth, stx_ref, sty_ref, stz_ref, obs_ref, cnt_ref, sum_ref, table
    )
    share = -(-blocks // (lines + 1))

    @pl.loop(1, lines + 2)
    def _(i):
        turn(i, False)

        @pl.loop(0, share)
        def _(j):
            step = (i - 1) * share + j
            pl.when(step < blocks)(lambda: tally(step))

    own_copy.wait()
    sends(me, True, True)
    for k in range(1, lines):
        own_line(k, True)

    @pl.loop(1, lines + 2)
    def _(i):
        turn(i, True)

    @pl.loop(0, bricks)
    def _(q):
        @pl.when(q != me)
        def _():
            remote(piece(q, 1 - h), piece(q, 1 - h), send_sem.at[2, q], twin_sem.at[q], twin, me).wait_recv()


def solve_kernel(
    pair_depth,
    sx_ref,
    sy_ref,
    sz_ref,
    stx_ref,
    sty_ref,
    stz_ref,
    slow_ref,
    cnt_ref,
    sum_ref,
    adj_ref,
    arr_ref,
    time,
    ping,
    pong,
    cost,
    picked,
    weight,
    supply,
    field,
):
    grid_x, cells_y, cells_z = slow_ref.shape
    rows = cells_y // 8
    shift = rows.bit_length() - 1
    brick = lax.axis_index("brick")
    parity = lax.rem(brick, 2)
    pair = brick // 2
    lane = lax.broadcasted_iota(jnp.int32, (8, cells_z), 1)
    sub = lax.broadcasted_iota(jnp.int32, (8, cells_z), 0)
    lane_first = lane == 0
    lane_last = lane == cells_z - 1
    sub_first = sub == 0
    sub_last = sub == 7
    half_z = cells_z // 2
    upper = lane >= half_z
    index_up = jnp.where(lane_last, half_z - 1, jnp.where(upper, lane - half_z + 1, lane + half_z))
    index_down = jnp.where(lane_first, half_z, jnp.where(upper, lane - half_z, lane + half_z - 1))
    split = jnp.where(upper, (lane - half_z) * 2 + 1, lane * 2)
    join = (lane & 1) * half_z + (lane >> 1)

    def layer_of(ref, x):
        return tuple(ref[x * rows + v] for v in range(rows))

    def y_up(cur, v):
        return cur[v + 1] if v + 1 < rows else pltpu.roll(cur[0], 7, 0)

    def y_down(cur, v):
        return cur[v - 1] if v else pltpu.roll(cur[rows - 1], 1, 0)

    def z_up(one):
        return jnp.take_along_axis(one, index_up, axis=1)

    def z_down(one):
        return jnp.take_along_axis(one, index_down, axis=1)

    def swap(a, b):
        moved = pltpu.roll(jnp.where(upper, a, b), half_z, 1)
        return jnp.where(upper, moved, a), jnp.where(upper, b, moved)

    half_x = grid_x // 2
    sx = sx_ref[parity]
    sy = sy_ref[parity]
    sz = sz_ref[parity]
    shift_x = jnp.where(upper, half_x, 0) - sx
    z_even = jnp.where(upper, lane - half_z, lane) * 2 - sz
    flat = []
    for odd in range(2):
        dz = (z_even + odd).astype(jnp.float32)
        for v in range(rows):
            dy = (sub * rows + v - sy).astype(jnp.float32)
            flat.append(dy * dy + dz * dz)

    def slot(x, odd, v):
        return (x * 2 + odd) * rows + v

    @pl.loop(0, half_x)
    def _(x):
        dx = (x + shift_x).astype(jnp.float32)
        dx = dx * dx
        for v in range(rows):
            near = jnp.take_along_axis(slow_ref[x, pl.ds(v, 8, stride=rows), :], split, axis=1)
            far = jnp.take_along_axis(slow_ref[x + half_x, pl.ds(v, 8, stride=rows), :], split, axis=1)
            for odd, slow in enumerate(swap(near, far)):
                start = (start_slowness * spacing) * jnp.sqrt(dx + flat[odd * rows + v])
                cost[slot(x, odd, v)] = (2.0 * half_step) * slow
                ping[slot(x + 1, odd, v)] = start + half_step * slow

    inner = jnp.where(upper, lane - half_z, lane)
    far_index = (
        jnp.where(inner == 0, lane, lane - 1),
        jnp.where(inner == half_z - 1, lane, lane + 1),
    )

    def sweep(src, dst):
        for odd in range(2):
            for v in range(rows):
                first = pltpu.roll(src[slot(1, odd, v)], half_z, 1)
                last = pltpu.roll(src[slot(half_x, odd, v)], half_z, 1)
                src[slot(0, odd, v)] = jnp.where(upper, last, big_value)
                src[slot(half_x + 1, odd, v)] = jnp.where(upper, big_value, first)

        @pl.loop(0, half_x // FORWARD)
        def _(i):
            for j in range(FORWARD):
                x = i * FORWARD + j
                cur = [[src[slot(x + 1, odd, v)] for v in range(rows)] for odd in range(2)]
                for v in range(rows):
                    for odd in range(2):
                        one = cur[odd][v]
                        pair_z = cur[1 - odd][v]
                        up = y_up(cur[odd], v)
                        down = y_down(cur[odd], v)
                        if v + 1 == rows:
                            up = jnp.where(sub_last, big_value, up)
                        if v == 0:
                            down = jnp.where(sub_first, big_value, down)
                        far_z = jnp.take_along_axis(pair_z, far_index[odd], axis=1)
                        along_x = jnp.minimum(src[slot(x, odd, v)], src[slot(x + 2, odd, v)])
                        low = jnp.minimum(
                            jnp.minimum(along_x, jnp.minimum(up, down)), jnp.minimum(pair_z, far_z)
                        )
                        dst[slot(x + 1, odd, v)] = jnp.minimum(one, low + cost[slot(x, odd, v)])

    assert ITERS % 2 == 0

    @pl.loop(0, ITERS // 2)
    def _(_step):
        sweep(ping, pong)
        sweep(pong, ping)

    @pl.loop(0, half_x)
    def _(x):
        for v in range(rows):
            even, odd = (ping[slot(x + 1, k, v)] - 0.5 * cost[slot(x, k, v)] for k in range(2))
            near, far = swap(even, odd)
            time[(x + 1) * rows + v] = near
            time[(x + half_x + 1) * rows + v] = far

    for v in range(rows):
        time[v] = jnp.full((8, cells_z), -big_value, jnp.float32)
        time[(grid_x + 1) * rows + v] = jnp.full((8, cells_z), -big_value, jnp.float32)

    count = picked.shape[0]
    line = lax.broadcasted_iota(jnp.int32, (1, cells_z), 1)
    unroll = 8

    @pl.loop(0, count // unroll)
    def _(i):
        for j in range(unroll):
            r = pair * count + i * unroll + j
            y = sty_ref[r]
            z = stz_ref[r]
            at = (stx_ref[r] + 1) * rows + (y & (rows - 1))
            got = time[at, pl.ds(y >> shift, 1), :]
            picked[pl.ds(i * unroll + j, 1), :] = jnp.where(line == (z & 1) * half_z + (z >> 1), got, 0.0)

    arrived = jnp.sum(jnp.transpose(picked[...]), axis=0, keepdims=True)
    arr_ref[0] = arrived[:, : count // 2]
    arr_ref[1] = arrived[:, count // 2 :]

    base, length = window(pair_depth, grid_x, ITERS - 1)
    outer, _ = window(pair_depth, grid_x, ITERS)

    def weigh(x, prev, cur):
        nxt = layer_of(time, x + 2)
        spot = (x - base) * rows
        for v in range(rows):
            one = cur[v]

            def gain(other):
                return jnp.maximum(other - one, 0.0)

            up = gain(y_up(cur, v))
            down = gain(y_down(cur, v))
            if v + 1 == rows:
                up = jnp.where(sub_last, 0.0, up)
            if v == 0:
                down = jnp.where(sub_first, 0.0, down)
            parts = (
                gain(prev[v]),
                gain(nxt[v]),
                down,
                up,
                jnp.where(lane_first, 0.0, gain(z_down(one))),
                jnp.where(lane_last, 0.0, gain(z_up(one))),
            )
            total = ((parts[0] + parts[1]) + (parts[2] + parts[3])) + (parts[4] + parts[5])
            inverse = 1.0 / (1.0 + total * (1.0 / spacing))
            scaled = inverse * (1.0 / spacing)
            for k, part in enumerate(parts):
                weight[k, spot + v] = part * scaled
            here = (x - outer) * rows + v
            value = (cnt_ref[here] * one - sum_ref[here]) * inverse
            supply[spot + v] = value
            field[spot + rows + v] = value
        return nxt

    def weigh_body(i, carry):
        prev, cur = carry
        for j in range(2):
            nxt = weigh(base + i * 2 + j, prev, cur)
            prev, cur = cur, nxt
        return prev, cur

    lax.fori_loop(0, length // 2, weigh_body, (layer_of(time, base), layer_of(time, base + 1)))
    for v in range(rows):
        field[v] = jnp.zeros((8, cells_z), jnp.float32)
        field[(length + 1) * rows + v] = jnp.zeros((8, cells_z), jnp.float32)

    def backward(x, prev, cur):
        nxt = layer_of(field, x + 2)
        for v in range(rows):
            one = cur[v]
            spot = x * rows + v
            acc = supply[spot] + weight[0, spot] * prev[v]
            acc = acc + weight[1, spot] * nxt[v]
            side = weight[2, spot] * y_down(cur, v) + weight[3, spot] * y_up(cur, v)
            acc = acc + side
            acc = acc + (weight[4, spot] * z_down(one) + weight[5, spot] * z_up(one))
            field[spot + rows] = acc
        return nxt

    @pl.loop(2, ITERS + 1)
    def _(sweep):
        margin = ITERS - sweep
        span = jnp.minimum(grid_x, (pair_depth + 2 * margin + BACKWARD - 1) // BACKWARD * BACKWARD)
        first = jnp.clip(pair * pair_depth - margin, 0, grid_x - span) - base

        def body(i, carry):
            prev, cur = carry
            for j in range(BACKWARD):
                nxt = backward(first + i * BACKWARD + j, prev, cur)
                prev, cur = cur, nxt
            return prev, cur

        lax.fori_loop(0, span // BACKWARD, body, (layer_of(field, first), layer_of(field, first + 1)))

    mine = pair * pair_depth - base + 1
    for x in range(pair_depth):
        for v in range(rows):
            adj_ref[x, pl.ds(v, 8, stride=rows), :] = jnp.take_along_axis(
                field[(mine + x) * rows + v], join, axis=1
            )


def reduce_kernel(cores, adj_ref, arr_ref, out_ref, got_ref, slots, send_sem, recv_sem, word_send, word_recv):
    depth, keep, _ = out_ref.shape
    brick = lax.axis_index("brick")
    core = lax.axis_index("src")
    parity = lax.rem(brick, 2)
    other = brick + 1 - 2 * parity
    me = core * 2 + parity

    def target(k):
        c = lax.rem(core + k // 2, cores)
        p = lax.rem(parity + k % 2, 2)
        return c, p, brick - parity + p

    def copy(k):
        c, p, b = target(k)
        return remote(
            adj_ref.at[pl.ds(p * depth, depth), pl.ds(c * keep, keep)],
            slots.at[k],
            send_sem.at[k],
            recv_sem.at[k],
            c,
            b,
        )

    barrier = pltpu.get_barrier_semaphore()
    for k in range(1, 2 * cores):
        c, _, b = target(k)
        pl.semaphore_signal(barrier, inc=1, device_id={"src": c, "brick": b}, device_id_type=MESH)
    pl.semaphore_wait(barrier, 2 * cores - 1)
    word = remote(arr_ref.at[1 - parity], got_ref.at[parity], word_send, word_recv, core, other)
    word.start()
    for k in range(1, 2 * cores):
        copy(k).start()
    got_ref[parity] = arr_ref[parity]
    total = adj_ref[pl.ds(parity * depth, depth), pl.ds(pl.multiple_of(core * keep, 8), keep), :]
    for k in range(1, 2 * cores):
        copy(k).wait_recv()
        total = total + slots[k]
    out_ref[...] = total
    for k in range(1, 2 * cores):
        copy(k).wait_send()
    word.wait_send()
    remote(arr_ref.at[parity], got_ref.at[1 - parity], word_send, word_recv, core, other).wait_recv()


def per_device(slowness, source_x, source_y, source_z, station_x, station_y, station_z, observed):
    bricks = lax.axis_size("brick")
    cores = lax.axis_size("src")
    depth, cells_y, cells_z = slowness.shape
    grid_x = depth * bricks
    rec = station_x.shape[0]
    pair_depth = 2 * depth
    rows = cells_y // 8
    assert source_x.shape[0] == 2 and bricks % LOW == 0 and cores % 2 == 0
    f32 = jnp.float32

    wide = min(grid_x, pair_depth + 2 * ITERS)
    field = jax.ShapeDtypeStruct((wide * rows, 8, cells_z), f32)
    full, cnt, total = pl.pallas_call(
        functools.partial(gather_kernel, bricks, pair_depth),
        name="gather",
        out_shape=(jax.ShapeDtypeStruct((grid_x, cells_y, cells_z), f32), field, field),
        in_specs=[VMEM] * 5,
        out_specs=(VMEM, VMEM, VMEM),
        scratch_shapes=[
            pltpu.VMEM((4 * cells_z, rec), jnp.bfloat16),
            pltpu.SemaphoreType.DMA((2, bricks // LOW)),
            pltpu.SemaphoreType.DMA((3, bricks)),
            pltpu.SemaphoreType.DMA((bricks,)),
            pltpu.SemaphoreType.DMA((bricks,)),
            pltpu.SemaphoreType.DMA,
        ],
        compiler_params=pltpu.CompilerParams(collective_id=0, has_side_effects=True),
    )(slowness, station_x[None], station_y[None], station_z[None], observed)

    length = min(grid_x, pair_depth + 2 * (ITERS - 1))
    share = rec // bricks
    adj, arr = pl.pallas_call(
        functools.partial(solve_kernel, pair_depth),
        name="solve",
        out_shape=(
            jax.ShapeDtypeStruct((pair_depth, cells_y, cells_z), f32),
            jax.ShapeDtypeStruct((2, 1, share), f32),
        ),
        in_specs=[SMEM] * 6 + [VMEM] * 3,
        out_specs=(VMEM, VMEM),
        scratch_shapes=[
            pltpu.VMEM(((grid_x + 2) * rows, 8, cells_z), f32),
            pltpu.VMEM(((grid_x + 4) * rows, 8, cells_z), f32),
            pltpu.VMEM(((grid_x + 4) * rows, 8, cells_z), f32),
            pltpu.VMEM((grid_x * rows, 8, cells_z), f32),
            pltpu.VMEM((2 * share, cells_z), f32),
            pltpu.VMEM((6, length * rows, 8, cells_z), f32),
            pltpu.VMEM((length * rows, 8, cells_z), f32),
            pltpu.VMEM(((length + 2) * rows, 8, cells_z), f32),
        ],
    )(source_x, source_y, source_z, station_x, station_y, station_z, full, cnt, total)

    keep = cells_y // cores
    summed, arrivals = pl.pallas_call(
        functools.partial(reduce_kernel, cores),
        name="reduce",
        out_shape=(
            jax.ShapeDtypeStruct((depth, keep, cells_z), f32),
            jax.ShapeDtypeStruct((2, 1, share), f32),
        ),
        in_specs=[VMEM, VMEM],
        out_specs=(VMEM, VMEM),
        scratch_shapes=[
            pltpu.VMEM((2 * cores, depth, keep, cells_z), f32),
            pltpu.SemaphoreType.DMA((2 * cores,)),
            pltpu.SemaphoreType.DMA((2 * cores,)),
            pltpu.SemaphoreType.DMA,
            pltpu.SemaphoreType.DMA,
        ],
        compiler_params=pltpu.CompilerParams(collective_id=1, has_side_effects=True),
    )(adj, arr)
    own = lax.dynamic_slice_in_dim(slowness, lax.axis_index("src") * keep, keep, axis=1)
    return own * summed, arrivals[:, 0]


def solution(mesh):
    in_specs = (P("brick", None, None), P("src"), P("src"), P("src"), P(), P(), P(), P("src", None))
    out_specs = (P("brick", "src", None), P("src", "brick"))
    return jax.shard_map(
        per_device, mesh=mesh, in_specs=in_specs, out_specs=out_specs, check_vma=False
    )
```

```python
import functools

import jax
import jax.numpy as jnp
from jax import lax
from jax.experimental import pallas as pl
from jax.experimental.pallas import tpu as pltpu
from jax.sharding import PartitionSpec as P

ITERS = 16

spacing = 0.015625
big_value = 1000000.0
start_slowness = 2.0
half_step = 0.5 * spacing
LOW = 4
FORWARD = 8
GATHER_VMEM = 24 << 20
SOLVE_VMEM = 40 << 20
REDUCE_VMEM = 8 << 20
BACKWARD = 4

VMEM = pl.BlockSpec(memory_space=pltpu.VMEM)
SMEM = pl.BlockSpec(memory_space=pltpu.SMEM)
MESH = pl.DeviceIdType.MESH


def remote(src, dst, send_sem, recv_sem, core, brick):
    return pltpu.make_async_remote_copy(
        src_ref=src,
        dst_ref=dst,
        send_sem=send_sem,
        recv_sem=recv_sem,
        device_id={"src": core, "brick": brick},
        device_id_type=MESH,
    )


def window(pair_depth, grid_x, margin):
    length = min(grid_x, pair_depth + 2 * margin)
    pair = lax.axis_index("brick") // 2
    return jnp.clip(pair * pair_depth - margin, 0, grid_x - length), length


def stations(grid_x, cells_y, pair_depth, stx_ref, sty_ref, stz_ref, obs_ref, cnt_ref, sum_ref, table):
    rec = stx_ref.shape[1]
    cells_z = cnt_ref.shape[2]
    rows_y = cells_y // 8
    shift = rows_y.bit_length() - 1
    low, length = window(pair_depth, grid_x, ITERS)
    parity = lax.rem(lax.axis_index("brick"), 2)
    sty = sty_ref[...]
    row = (stx_ref[...] - low) * cells_y + (sty & (rows_y - 1)) * 8 + (sty >> shift)
    seen = obs_ref[pl.ds(parity, 1), :]
    hi = seen.astype(jnp.bfloat16).astype(jnp.float32)
    rest = seen - hi
    mid = rest.astype(jnp.bfloat16).astype(jnp.float32)
    lo = rest - mid
    stz = stz_ref[...]
    hit = lax.broadcasted_iota(jnp.int32, (cells_z, rec), 0) == (stz & 1) * (cells_z // 2) + (stz >> 1)
    for part, value in enumerate((jnp.ones_like(seen), hi, mid, lo)):
        table[pl.ds(part * cells_z, cells_z), :] = jnp.where(hit, value, 0.0).astype(jnp.bfloat16)
    block = 256
    tiles = block // 8

    def tally(step):
        rows = lax.broadcasted_iota(jnp.int32, (block, rec), 0) + step * block
        pick = jnp.where(rows == row, 1.0, 0.0).astype(jnp.bfloat16)
        got = lax.dot_general(
            pick, table[...], (((1,), (1,)), ((), ())), preferred_element_type=jnp.float32
        )
        cnt_ref[pl.ds(step * tiles, tiles)] = got[:, :cells_z].reshape(tiles, 8, cells_z)
        total = got[:, cells_z : 2 * cells_z] + (
            got[:, 2 * cells_z : 3 * cells_z] + got[:, 3 * cells_z :]
        )
        sum_ref[pl.ds(step * tiles, tiles)] = total.reshape(tiles, 8, cells_z)

    return length * cells_y // block, tally


def gather_kernel(
    bricks,
    pair_depth,
    slow_ref,
    stx_ref,
    sty_ref,
    stz_ref,
    obs_ref,
    full_ref,
    cnt_ref,
    sum_ref,
    table,
    line_sem,
    send_sem,
    recv_sem,
    twin_sem,
    own_sem,
):
    depth = slow_ref.shape[0]
    half = depth // 2
    lines = bricks // LOW
    me = lax.axis_index("brick")
    core = lax.axis_index("src")
    h = lax.rem(core, 2)
    twin = core + 1 - 2 * h
    line = me // LOW
    bit_x = lax.rem(me, 2)
    bit_y = lax.rem(me // 2, 2)
    flip_x = 1 - 2 * bit_x
    flip_y = 2 - 4 * bit_y
    first = me + flip_x * (1 - h) + flip_y * h
    second = me + flip_y * (1 - h) + flip_x * h
    corner = me + flip_x + flip_y

    def piece(q, part):
        return full_ref.at[pl.ds(q * depth + part * half, half)]

    def copy(kind, q, brick, own=False):
        src = slow_ref.at[pl.ds(h * half, half)] if own else piece(q, h)
        return remote(src, piece(q, h), send_sem.at[kind, q], recv_sem.at[q], core, brick)

    def twin_copy(q):
        return remote(piece(q, h), piece(q, h), send_sem.at[2, q], twin_sem.at[q], twin, me)

    barrier = pltpu.get_barrier_semaphore()

    def greet(c, b):
        pl.semaphore_signal(barrier, inc=1, device_id={"src": c, "brick": b}, device_id_type=MESH)

    greet(twin, me)
    greet(core, first)
    greet(core, second)
    for k in range(1, lines):
        pl.when(line >= k)(lambda k=k: greet(core, me - LOW * k))
        pl.when(line + k < lines)(lambda k=k: greet(core, me + LOW * k))
    pl.semaphore_wait(barrier, lines + 2)

    def along(k, up):
        dst = piece(me, h)
        src = slow_ref.at[pl.ds(h * half, half)]
        brick = me + LOW * k if up else me - LOW * k
        return remote(src, dst, line_sem.at[int(up), k], recv_sem.at[me], core, brick)

    def own_line(k, wait):
        def go(up):
            c = along(k, up)
            c.wait_send() if wait else c.start()

        pl.when(line >= k)(lambda: go(False))
        pl.when(line + k < lines)(lambda: go(True))

    def sends(q, own, wait):
        for kind, brick in ((0, first), (1, second)):
            c = copy(kind, q, brick, own)
            c.wait_send() if wait else c.start()

    own_copy = pltpu.make_async_copy(slow_ref, full_ref.at[pl.ds(me * depth, depth)], own_sem)
    for k in range(1, lines):
        own_line(k, False)
        if k == 1:
            sends(me, True, False)
    own_copy.start()

    def arrived(q):
        remote(piece(q, h), piece(q, h), send_sem.at[0, q], recv_sem.at[q], core, first).wait_recv()

    def on_line(base, i, act):
        pl.when((i < lines) & (line >= i))(lambda: act(base - LOW * i, -1))
        pl.when((i < lines) & (line + i < lines))(lambda: act(base + LOW * i, 1))

    def both(base, i, act):
        pl.when(i == 0)(lambda: act(base, 0))
        pl.when(i > 0)(lambda: on_line(base, i, act))

    def from_line(wait):
        def act(q, side):
            if not wait:
                arrived(q)
            sends(q, False, wait)
            c = twin_copy(q)
            c.wait_send() if wait else c.start()

        return act

    def from_first(wait):
        def act(q, side):
            if not wait:
                arrived(q)
            c = copy(1, q, second)
            c.wait_send() if wait else c.start()
            c = twin_copy(q)
            c.wait_send() if wait else c.start()

        return act

    def from_second(wait):
        def act(q, side):
            if not wait:
                arrived(q)
            c = twin_copy(q)
            c.wait_send() if wait else c.start()

        return act

    def turn(i, wait):
        on_line(me, i, from_line(wait))
        both(first, i - 1, from_first(wait))
        both(second, i - 1, from_second(wait))
        pl.when(i >= 2)(lambda: both(corner, i - 2, from_second(wait)))

    grid_x, cells_y, _ = full_ref.shape
    blocks, tally = stations(
        grid_x, cells_y, pair_depth, stx_ref, sty_ref, stz_ref, obs_ref, cnt_ref, sum_ref, table
    )
    early = 2
    rounds = lines + 1

    @pl.loop(0, early + rounds)
    def _(step):
        pl.when(step < blocks)(lambda: tally(step))
        pl.when(step >= early)(lambda: turn(step - early + 1, False))

    @pl.loop(early + rounds, max(blocks, early + rounds))
    def _(step):
        tally(step)

    own_copy.wait()
    sends(me, True, True)
    for k in range(1, lines):
        own_line(k, True)

    @pl.loop(1, lines + 2)
    def _(i):
        turn(i, True)

    @pl.loop(0, bricks)
    def _(q):
        @pl.when(q != me)
        def _():
            remote(piece(q, 1 - h), piece(q, 1 - h), send_sem.at[2, q], twin_sem.at[q], twin, me).wait_recv()


def solve_kernel(
    pair_depth,
    sx_ref,
    sy_ref,
    sz_ref,
    stx_ref,
    sty_ref,
    stz_ref,
    slow_ref,
    cnt_ref,
    sum_ref,
    adj_ref,
    arr_ref,
    time,
    ping,
    pong,
    cost,
    picked,
    weight,
    supply,
    field,
):
    grid_x, cells_y, cells_z = slow_ref.shape
    rows = cells_y // 8
    shift = rows.bit_length() - 1
    brick = lax.axis_index("brick")
    parity = lax.rem(brick, 2)
    pair = brick // 2
    lane = lax.broadcasted_iota(jnp.int32, (8, cells_z), 1)
    sub = lax.broadcasted_iota(jnp.int32, (8, cells_z), 0)
    lane_first = lane == 0
    lane_last = lane == cells_z - 1
    sub_first = sub == 0
    sub_last = sub == 7
    half_z = cells_z // 2
    upper = lane >= half_z
    index_up = jnp.where(lane_last, half_z - 1, jnp.where(upper, lane - half_z + 1, lane + half_z))
    index_down = jnp.where(lane_first, half_z, jnp.where(upper, lane - half_z, lane + half_z - 1))
    split = jnp.where(upper, (lane - half_z) * 2 + 1, lane * 2)
    join = (lane & 1) * half_z + (lane >> 1)

    def layer_of(ref, x):
        return tuple(ref[x * rows + v] for v in range(rows))

    def y_up(cur, v):
        return cur[v + 1] if v + 1 < rows else pltpu.roll(cur[0], 7, 0)

    def y_down(cur, v):
        return cur[v - 1] if v else pltpu.roll(cur[rows - 1], 1, 0)

    def z_up(one):
        return jnp.take_along_axis(one, index_up, axis=1)

    def z_down(one):
        return jnp.take_along_axis(one, index_down, axis=1)

    def swap(a, b):
        moved = pltpu.roll(jnp.where(upper, a, b), half_z, 1)
        return jnp.where(upper, moved, a), jnp.where(upper, b, moved)

    half_x = grid_x // 2
    sx = sx_ref[parity]
    sy = sy_ref[parity]
    sz = sz_ref[parity]
    shift_x = jnp.where(upper, half_x, 0) - sx
    z_even = jnp.where(upper, lane - half_z, lane) * 2 - sz
    flat = []
    for odd in range(2):
        dz = (z_even + odd).astype(jnp.float32)
        for v in range(rows):
            dy = (sub * rows + v - sy).astype(jnp.float32)
            flat.append(dy * dy + dz * dz)

    def slot(x, odd, v):
        return (x * 2 + odd) * rows + v

    @pl.loop(0, half_x)
    def _(x):
        dx = (x + shift_x).astype(jnp.float32)
        dx = dx * dx
        for v in range(rows):
            near = jnp.take_along_axis(slow_ref[x, pl.ds(v, 8, stride=rows), :], split, axis=1)
            far = jnp.take_along_axis(slow_ref[x + half_x, pl.ds(v, 8, stride=rows), :], split, axis=1)
            for odd, slow in enumerate(swap(near, far)):
                start = (start_slowness * spacing) * jnp.sqrt(dx + flat[odd * rows + v])
                cost[slot(x, odd, v)] = (2.0 * half_step) * slow
                ping[slot(x + 1, odd, v)] = start + half_step * slow

    inner = jnp.where(upper, lane - half_z, lane)
    far_index = (
        jnp.where(inner == 0, lane, lane - 1),
        jnp.where(inner == half_z - 1, lane, lane + 1),
    )

    def sweep(src, dst):
        for odd in range(2):
            for v in range(rows):
                first = pltpu.roll(src[slot(1, odd, v)], half_z, 1)
                last = pltpu.roll(src[slot(half_x, odd, v)], half_z, 1)
                src[slot(0, odd, v)] = jnp.where(upper, last, big_value)
                src[slot(half_x + 1, odd, v)] = jnp.where(upper, big_value, first)

        @pl.loop(0, half_x // FORWARD)
        def _(i):
            for j in range(FORWARD):
                x = i * FORWARD + j
                cur = [[src[slot(x + 1, odd, v)] for v in range(rows)] for odd in range(2)]
                for v in range(rows):
                    for odd in range(2):
                        one = cur[odd][v]
                        pair_z = cur[1 - odd][v]
                        up = y_up(cur[odd], v)
                        down = y_down(cur[odd], v)
                        if v + 1 == rows:
                            up = jnp.where(sub_last, big_value, up)
                        if v == 0:
                            down = jnp.where(sub_first, big_value, down)
                        far_z = jnp.take_along_axis(pair_z, far_index[odd], axis=1)
                        along_x = jnp.minimum(src[slot(x, odd, v)], src[slot(x + 2, odd, v)])
                        low = jnp.minimum(
                            jnp.minimum(along_x, jnp.minimum(up, down)), jnp.minimum(pair_z, far_z)
                        )
                        dst[slot(x + 1, odd, v)] = jnp.minimum(one, low + cost[slot(x, odd, v)])

    assert ITERS % 2 == 0

    @pl.loop(0, ITERS // 2)
    def _(_step):
        sweep(ping, pong)
        sweep(pong, ping)

    @pl.loop(0, half_x)
    def _(x):
        for v in range(rows):
            even, odd = (ping[slot(x + 1, k, v)] - 0.5 * cost[slot(x, k, v)] for k in range(2))
            near, far = swap(even, odd)
            time[(x + 1) * rows + v] = near
            time[(x + half_x + 1) * rows + v] = far

    for v in range(rows):
        time[v] = jnp.full((8, cells_z), -big_value, jnp.float32)
        time[(grid_x + 1) * rows + v] = jnp.full((8, cells_z), -big_value, jnp.float32)

    count = picked.shape[0]
    line = lax.broadcasted_iota(jnp.int32, (1, cells_z), 1)
    unroll = 8

    @pl.loop(0, count // unroll)
    def _(i):
        for j in range(unroll):
            r = pair * count + i * unroll + j
            y = sty_ref[r]
            z = stz_ref[r]
            at = (stx_ref[r] + 1) * rows + (y & (rows - 1))
            got = time[at, pl.ds(y >> shift, 1), :]
            picked[pl.ds(i * unroll + j, 1), :] = jnp.where(line == (z & 1) * half_z + (z >> 1), got, 0.0)

    arrived = jnp.sum(jnp.transpose(picked[...]), axis=0, keepdims=True)
    arr_ref[0] = arrived[:, : count // 2]
    arr_ref[1] = arrived[:, count // 2 :]

    base, length = window(pair_depth, grid_x, ITERS - 1)
    outer, _ = window(pair_depth, grid_x, ITERS)

    def weigh(x, prev, cur):
        nxt = layer_of(time, x + 2)
        spot = (x - base) * rows
        for v in range(rows):
            one = cur[v]

            def gain(other):
                return jnp.maximum(other - one, 0.0)

            up = gain(y_up(cur, v))
            down = gain(y_down(cur, v))
            if v + 1 == rows:
                up = jnp.where(sub_last, 0.0, up)
            if v == 0:
                down = jnp.where(sub_first, 0.0, down)
            parts = (
                gain(prev[v]),
                gain(nxt[v]),
                down,
                up,
                jnp.where(lane_first, 0.0, gain(z_down(one))),
                jnp.where(lane_last, 0.0, gain(z_up(one))),
            )
            total = ((parts[0] + parts[1]) + (parts[2] + parts[3])) + (parts[4] + parts[5])
            inverse = 1.0 / (1.0 + total * (1.0 / spacing))
            scaled = inverse * (1.0 / spacing)
            for k, part in enumerate(parts):
                weight[k, spot + v] = part * scaled
            here = (x - outer) * rows + v
            value = (cnt_ref[here] * one - sum_ref[here]) * inverse
            supply[spot + v] = value
            field[spot + rows + v] = value
        return nxt

    def weigh_body(i, carry):
        prev, cur = carry
        for j in range(2):
            nxt = weigh(base + i * 2 + j, prev, cur)
            prev, cur = cur, nxt
        return prev, cur

    lax.fori_loop(0, length // 2, weigh_body, (layer_of(time, base), layer_of(time, base + 1)))
    for v in range(rows):
        field[v] = jnp.zeros((8, cells_z), jnp.float32)
        field[(length + 1) * rows + v] = jnp.zeros((8, cells_z), jnp.float32)

    def backward(x, prev, cur):
        nxt = layer_of(field, x + 2)
        for v in range(rows):
            one = cur[v]
            spot = x * rows + v
            acc = supply[spot] + weight[0, spot] * prev[v]
            acc = acc + weight[1, spot] * nxt[v]
            side = weight[2, spot] * y_down(cur, v) + weight[3, spot] * y_up(cur, v)
            acc = acc + side
            acc = acc + (weight[4, spot] * z_down(one) + weight[5, spot] * z_up(one))
            field[spot + rows] = acc
        return nxt

    @pl.loop(2, ITERS + 1)
    def _(sweep):
        margin = ITERS - sweep
        span = jnp.minimum(grid_x, (pair_depth + 2 * margin + BACKWARD - 1) // BACKWARD * BACKWARD)
        first = jnp.clip(pair * pair_depth - margin, 0, grid_x - span) - base

        def body(i, carry):
            prev, cur = carry
            for j in range(BACKWARD):
                nxt = backward(first + i * BACKWARD + j, prev, cur)
                prev, cur = cur, nxt
            return prev, cur

        lax.fori_loop(0, span // BACKWARD, body, (layer_of(field, first), layer_of(field, first + 1)))

    mine = pair * pair_depth - base + 1
    for x in range(pair_depth):
        for v in range(rows):
            adj_ref[x, pl.ds(v, 8, stride=rows), :] = jnp.take_along_axis(
                field[(mine + x) * rows + v], join, axis=1
            )


def reduce_kernel(cores, adj_ref, arr_ref, out_ref, got_ref, slots, send_sem, recv_sem, word_send, word_recv):
    depth, keep, _ = out_ref.shape
    brick = lax.axis_index("brick")
    core = lax.axis_index("src")
    parity = lax.rem(brick, 2)
    other = brick + 1 - 2 * parity
    me = core * 2 + parity

    def target(k):
        c = lax.rem(core + k // 2, cores)
        p = lax.rem(parity + k % 2, 2)
        return c, p, brick - parity + p

    def copy(k):
        c, p, b = target(k)
        return remote(
            adj_ref.at[pl.ds(p * depth, depth), pl.ds(c * keep, keep)],
            slots.at[k],
            send_sem.at[k],
            recv_sem.at[k],
            c,
            b,
        )

    barrier = pltpu.get_barrier_semaphore()
    for k in range(1, 2 * cores):
        c, _, b = target(k)
        pl.semaphore_signal(barrier, inc=1, device_id={"src": c, "brick": b}, device_id_type=MESH)
    pl.semaphore_wait(barrier, 2 * cores - 1)
    word = remote(arr_ref.at[1 - parity], got_ref.at[parity], word_send, word_recv, core, other)
    word.start()
    for k in range(1, 2 * cores):
        copy(k).start()
    got_ref[parity] = arr_ref[parity]
    total = adj_ref[pl.ds(parity * depth, depth), pl.ds(pl.multiple_of(core * keep, 8), keep), :]
    for k in range(1, 2 * cores):
        copy(k).wait_recv()
        total = total + slots[k]
    out_ref[...] = total
    for k in range(1, 2 * cores):
        copy(k).wait_send()
    word.wait_send()
    remote(arr_ref.at[parity], got_ref.at[1 - parity], word_send, word_recv, core, other).wait_recv()


def per_device(slowness, source_x, source_y, source_z, station_x, station_y, station_z, observed):
    bricks = lax.axis_size("brick")
    cores = lax.axis_size("src")
    depth, cells_y, cells_z = slowness.shape
    grid_x = depth * bricks
    rec = station_x.shape[0]
    pair_depth = 2 * depth
    rows = cells_y // 8
    assert source_x.shape[0] == 2 and bricks % LOW == 0 and cores % 2 == 0
    f32 = jnp.float32

    wide = min(grid_x, pair_depth + 2 * ITERS)
    field = jax.ShapeDtypeStruct((wide * rows, 8, cells_z), f32)
    full, cnt, total = pl.pallas_call(
        functools.partial(gather_kernel, bricks, pair_depth),
        name="gather",
        out_shape=(jax.ShapeDtypeStruct((grid_x, cells_y, cells_z), f32), field, field),
        in_specs=[VMEM] * 5,
        out_specs=(VMEM, VMEM, VMEM),
        scratch_shapes=[
            pltpu.VMEM((4 * cells_z, rec), jnp.bfloat16),
            pltpu.SemaphoreType.DMA((2, bricks // LOW)),
            pltpu.SemaphoreType.DMA((3, bricks)),
            pltpu.SemaphoreType.DMA((bricks,)),
            pltpu.SemaphoreType.DMA((bricks,)),
            pltpu.SemaphoreType.DMA,
        ],
        compiler_params=pltpu.CompilerParams(
            collective_id=0, has_side_effects=True, vmem_limit_bytes=GATHER_VMEM
        ),
    )(slowness, station_x[None], station_y[None], station_z[None], observed)

    length = min(grid_x, pair_depth + 2 * (ITERS - 1))
    share = rec // bricks
    adj, arr = pl.pallas_call(
        functools.partial(solve_kernel, pair_depth),
        name="solve",
        out_shape=(
            jax.ShapeDtypeStruct((pair_depth, cells_y, cells_z), f32),
            jax.ShapeDtypeStruct((2, 1, share), f32),
        ),
        in_specs=[SMEM] * 6 + [VMEM] * 3,
        out_specs=(VMEM, VMEM),
        scratch_shapes=[
            pltpu.VMEM(((grid_x + 2) * rows, 8, cells_z), f32),
            pltpu.VMEM(((grid_x + 4) * rows, 8, cells_z), f32),
            pltpu.VMEM(((grid_x + 4) * rows, 8, cells_z), f32),
            pltpu.VMEM((grid_x * rows, 8, cells_z), f32),
            pltpu.VMEM((2 * share, cells_z), f32),
            pltpu.VMEM((6, length * rows, 8, cells_z), f32),
            pltpu.VMEM((length * rows, 8, cells_z), f32),
            pltpu.VMEM(((length + 2) * rows, 8, cells_z), f32),
        ],
        compiler_params=pltpu.CompilerParams(vmem_limit_bytes=SOLVE_VMEM),
    )(source_x, source_y, source_z, station_x, station_y, station_z, full, cnt, total)

    keep = cells_y // cores
    summed, arrivals = pl.pallas_call(
        functools.partial(reduce_kernel, cores),
        name="reduce",
        out_shape=(
            jax.ShapeDtypeStruct((depth, keep, cells_z), f32),
            jax.ShapeDtypeStruct((2, 1, share), f32),
        ),
        in_specs=[VMEM, VMEM],
        out_specs=(VMEM, VMEM),
        scratch_shapes=[
            pltpu.VMEM((2 * cores, depth, keep, cells_z), f32),
            pltpu.SemaphoreType.DMA((2 * cores,)),
            pltpu.SemaphoreType.DMA((2 * cores,)),
            pltpu.SemaphoreType.DMA,
            pltpu.SemaphoreType.DMA,
        ],
        compiler_params=pltpu.CompilerParams(
            collective_id=1, has_side_effects=True, vmem_limit_bytes=REDUCE_VMEM
        ),
    )(adj, arr)
    own = lax.dynamic_slice_in_dim(slowness, lax.axis_index("src") * keep, keep, axis=1)
    return own * summed, arrivals[:, 0]


def solution(mesh):
    in_specs = (P("brick", None, None), P("src"), P("src"), P("src"), P(), P(), P(), P("src", None))
    out_specs = (P("brick", "src", None), P("src", "brick"))
    return jax.shard_map(
        per_device, mesh=mesh, in_specs=in_specs, out_specs=out_specs, check_vma=False
    )
```

```python
import functools

import jax
import jax.numpy as jnp
from jax import lax
from jax.experimental import pallas as pl
from jax.experimental.pallas import tpu as pltpu
from jax.sharding import PartitionSpec as P

ITERS = 16

spacing = 0.015625
big_value = 1000000.0
start_slowness = 2.0
half_step = 0.5 * spacing
LOW = 4
FORWARD = 8
GATHER_VMEM = 24 << 20
SOLVE_VMEM = 40 << 20
REDUCE_VMEM = 8 << 20
BACKWARD = 4

VMEM = pl.BlockSpec(memory_space=pltpu.VMEM)
SMEM = pl.BlockSpec(memory_space=pltpu.SMEM)
HBM = pl.BlockSpec(memory_space=pltpu.HBM)
MESH = pl.DeviceIdType.MESH


def remote(src, dst, send_sem, recv_sem, core, brick):
    return pltpu.make_async_remote_copy(
        src_ref=src,
        dst_ref=dst,
        send_sem=send_sem,
        recv_sem=recv_sem,
        device_id={"src": core, "brick": brick},
        device_id_type=MESH,
    )


def window(pair_depth, grid_x, margin):
    length = min(grid_x, pair_depth + 2 * margin)
    pair = lax.axis_index("brick") // 2
    return jnp.clip(pair * pair_depth - margin, 0, grid_x - length), length


def stations(grid_x, cells_y, pair_depth, stx_ref, sty_ref, stz_ref, obs_ref, cnt_ref, sum_ref, table):
    rec = stx_ref.shape[1]
    cells_z = cnt_ref.shape[2]
    rows_y = cells_y // 8
    shift = rows_y.bit_length() - 1
    low, length = window(pair_depth, grid_x, ITERS)
    parity = lax.rem(lax.axis_index("brick"), 2)
    sty = sty_ref[...]
    row = (stx_ref[...] - low) * cells_y + (sty & (rows_y - 1)) * 8 + (sty >> shift)
    seen = obs_ref[pl.ds(parity, 1), :]
    hi = seen.astype(jnp.bfloat16).astype(jnp.float32)
    rest = seen - hi
    mid = rest.astype(jnp.bfloat16).astype(jnp.float32)
    lo = rest - mid
    stz = stz_ref[...]
    hit = lax.broadcasted_iota(jnp.int32, (cells_z, rec), 0) == (stz & 1) * (cells_z // 2) + (stz >> 1)
    for part, value in enumerate((jnp.ones_like(seen), hi, mid, lo)):
        table[pl.ds(part * cells_z, cells_z), :] = jnp.where(hit, value, 0.0).astype(jnp.bfloat16)
    block = 256
    tiles = block // 8

    def tally(step):
        rows = lax.broadcasted_iota(jnp.int32, (block, rec), 0) + step * block
        pick = jnp.where(rows == row, 1.0, 0.0).astype(jnp.bfloat16)
        got = lax.dot_general(
            pick, table[...], (((1,), (1,)), ((), ())), preferred_element_type=jnp.float32
        )
        cnt_ref[pl.ds(step * tiles, tiles)] = got[:, :cells_z].reshape(tiles, 8, cells_z)
        total = got[:, cells_z : 2 * cells_z] + (
            got[:, 2 * cells_z : 3 * cells_z] + got[:, 3 * cells_z :]
        )
        sum_ref[pl.ds(step * tiles, tiles)] = total.reshape(tiles, 8, cells_z)

    return length * cells_y // block, tally


def gather_kernel(
    bricks,
    pair_depth,
    slow_ref,
    stx_ref,
    sty_ref,
    stz_ref,
    obs_ref,
    full_ref,
    cnt_ref,
    sum_ref,
    table,
    line_sem,
    send_sem,
    recv_sem,
    twin_sem,
    own_sem,
    stx_buf,
    sty_buf,
    stz_buf,
    obs_buf,
    in_sem,
):
    loads = [
        pltpu.make_async_copy(src, dst, in_sem.at[k])
        for k, (src, dst) in enumerate(
            ((stx_ref, stx_buf), (sty_ref, sty_buf), (stz_ref, stz_buf), (obs_ref, obs_buf))
        )
    ]
    for load in loads:
        load.start()
    depth = slow_ref.shape[0]
    half = depth // 2
    lines = bricks // LOW
    me = lax.axis_index("brick")
    core = lax.axis_index("src")
    h = lax.rem(core, 2)
    twin = core + 1 - 2 * h
    line = me // LOW
    bit_x = lax.rem(me, 2)
    bit_y = lax.rem(me // 2, 2)
    flip_x = 1 - 2 * bit_x
    flip_y = 2 - 4 * bit_y
    first = me + flip_x * (1 - h) + flip_y * h
    second = me + flip_y * (1 - h) + flip_x * h
    corner = me + flip_x + flip_y

    def piece(q, part):
        return full_ref.at[pl.ds(q * depth + part * half, half)]

    def copy(kind, q, brick, own=False):
        src = slow_ref.at[pl.ds(h * half, half)] if own else piece(q, h)
        return remote(src, piece(q, h), send_sem.at[kind, q], recv_sem.at[q], core, brick)

    def twin_copy(q):
        return remote(piece(q, h), piece(q, h), send_sem.at[2, q], twin_sem.at[q], twin, me)

    barrier = pltpu.get_barrier_semaphore()

    def greet(c, b):
        pl.semaphore_signal(barrier, inc=1, device_id={"src": c, "brick": b}, device_id_type=MESH)

    greet(twin, me)
    greet(core, first)
    greet(core, second)
    for k in range(1, lines):
        pl.when(line >= k)(lambda k=k: greet(core, me - LOW * k))
        pl.when(line + k < lines)(lambda k=k: greet(core, me + LOW * k))
    pl.semaphore_wait(barrier, lines + 2)

    def along(k, up):
        dst = piece(me, h)
        src = slow_ref.at[pl.ds(h * half, half)]
        brick = me + LOW * k if up else me - LOW * k
        return remote(src, dst, line_sem.at[int(up), k], recv_sem.at[me], core, brick)

    def own_line(k, wait):
        def go(up):
            c = along(k, up)
            c.wait_send() if wait else c.start()

        pl.when(line >= k)(lambda: go(False))
        pl.when(line + k < lines)(lambda: go(True))

    def sends(q, own, wait):
        for kind, brick in ((0, first), (1, second)):
            c = copy(kind, q, brick, own)
            c.wait_send() if wait else c.start()

    own_copy = pltpu.make_async_copy(slow_ref, full_ref.at[pl.ds(me * depth, depth)], own_sem)
    for k in range(1, lines):
        own_line(k, False)
        if k == 1:
            sends(me, True, False)
    own_copy.start()

    def arrived(q):
        remote(piece(q, h), piece(q, h), send_sem.at[0, q], recv_sem.at[q], core, first).wait_recv()

    def on_line(base, i, act):
        pl.when((i < lines) & (line >= i))(lambda: act(base - LOW * i, -1))
        pl.when((i < lines) & (line + i < lines))(lambda: act(base + LOW * i, 1))

    def both(base, i, act):
        pl.when(i == 0)(lambda: act(base, 0))
        pl.when(i > 0)(lambda: on_line(base, i, act))

    def from_line(wait):
        def act(q, side):
            if not wait:
                arrived(q)
            sends(q, False, wait)
            c = twin_copy(q)
            c.wait_send() if wait else c.start()

        return act

    def from_first(wait):
        def act(q, side):
            if not wait:
                arrived(q)
            c = copy(1, q, second)
            c.wait_send() if wait else c.start()
            c = twin_copy(q)
            c.wait_send() if wait else c.start()

        return act

    def from_second(wait):
        def act(q, side):
            if not wait:
                arrived(q)
            c = twin_copy(q)
            c.wait_send() if wait else c.start()

        return act

    def turn(i, wait):
        on_line(me, i, from_line(wait))
        both(first, i - 1, from_first(wait))
        both(second, i - 1, from_second(wait))
        pl.when(i >= 2)(lambda: both(corner, i - 2, from_second(wait)))

    grid_x, cells_y, _ = full_ref.shape
    for load in loads:
        load.wait()
    blocks, tally = stations(
        grid_x, cells_y, pair_depth, stx_buf, sty_buf, stz_buf, obs_buf, cnt_ref, sum_ref, table
    )
    early = 2
    rounds = lines + 1

    @pl.loop(0, early + rounds)
    def _(step):
        pl.when(step < blocks)(lambda: tally(step))
        pl.when(step >= early)(lambda: turn(step - early + 1, False))

    @pl.loop(early + rounds, max(blocks, early + rounds))
    def _(step):
        tally(step)

    own_copy.wait()
    sends(me, True, True)
    for k in range(1, lines):
        own_line(k, True)

    @pl.loop(1, lines + 2)
    def _(i):
        turn(i, True)

    @pl.loop(0, bricks)
    def _(q):
        @pl.when(q != me)
        def _():
            remote(piece(q, 1 - h), piece(q, 1 - h), send_sem.at[2, q], twin_sem.at[q], twin, me).wait_recv()


def solve_kernel(
    pair_depth,
    sx_ref,
    sy_ref,
    sz_ref,
    stx_hbm,
    sty_hbm,
    stz_hbm,
    slow_ref,
    cnt_ref,
    sum_ref,
    adj_ref,
    arr_ref,
    time,
    ping,
    pong,
    cost,
    picked,
    weight,
    supply,
    field,
    stx_ref,
    sty_ref,
    stz_ref,
    in_sem,
):
    loads = [
        pltpu.make_async_copy(src, dst, in_sem.at[k])
        for k, (src, dst) in enumerate(((stx_hbm, stx_ref), (sty_hbm, sty_ref), (stz_hbm, stz_ref)))
    ]
    for load in loads:
        load.start()
    grid_x, cells_y, cells_z = slow_ref.shape
    rows = cells_y // 8
    shift = rows.bit_length() - 1
    brick = lax.axis_index("brick")
    parity = lax.rem(brick, 2)
    pair = brick // 2
    lane = lax.broadcasted_iota(jnp.int32, (8, cells_z), 1)
    sub = lax.broadcasted_iota(jnp.int32, (8, cells_z), 0)
    lane_first = lane == 0
    lane_last = lane == cells_z - 1
    sub_first = sub == 0
    sub_last = sub == 7
    half_z = cells_z // 2
    upper = lane >= half_z
    index_up = jnp.where(lane_last, half_z - 1, jnp.where(upper, lane - half_z + 1, lane + half_z))
    index_down = jnp.where(lane_first, half_z, jnp.where(upper, lane - half_z, lane + half_z - 1))
    split = jnp.where(upper, (lane - half_z) * 2 + 1, lane * 2)
    join = (lane & 1) * half_z + (lane >> 1)

    def layer_of(ref, x):
        return tuple(ref[x * rows + v] for v in range(rows))

    def y_up(cur, v):
        return cur[v + 1] if v + 1 < rows else pltpu.roll(cur[0], 7, 0)

    def y_down(cur, v):
        return cur[v - 1] if v else pltpu.roll(cur[rows - 1], 1, 0)

    def z_up(one):
        return jnp.take_along_axis(one, index_up, axis=1)

    def z_down(one):
        return jnp.take_along_axis(one, index_down, axis=1)

    def swap(a, b):
        moved = pltpu.roll(jnp.where(upper, a, b), half_z, 1)
        return jnp.where(upper, moved, a), jnp.where(upper, b, moved)

    half_x = grid_x // 2
    sx = sx_ref[parity]
    sy = sy_ref[parity]
    sz = sz_ref[parity]
    shift_x = jnp.where(upper, half_x, 0) - sx
    z_even = jnp.where(upper, lane - half_z, lane) * 2 - sz
    flat = []
    for odd in range(2):
        dz = (z_even + odd).astype(jnp.float32)
        for v in range(rows):
            dy = (sub * rows + v - sy).astype(jnp.float32)
            flat.append(dy * dy + dz * dz)

    def slot(x, odd, v):
        return (x * 2 + odd) * rows + v

    @pl.loop(0, half_x)
    def _(x):
        dx = (x + shift_x).astype(jnp.float32)
        dx = dx * dx
        for v in range(rows):
            near = jnp.take_along_axis(slow_ref[x, pl.ds(v, 8, stride=rows), :], split, axis=1)
            far = jnp.take_along_axis(slow_ref[x + half_x, pl.ds(v, 8, stride=rows), :], split, axis=1)
            for odd, slow in enumerate(swap(near, far)):
                start = (start_slowness * spacing) * jnp.sqrt(dx + flat[odd * rows + v])
                cost[slot(x, odd, v)] = (2.0 * half_step) * slow
                ping[slot(x + 1, odd, v)] = start + half_step * slow

    inner = jnp.where(upper, lane - half_z, lane)
    far_index = (
        jnp.where(inner == 0, lane, lane - 1),
        jnp.where(inner == half_z - 1, lane, lane + 1),
    )

    def sweep(src, dst):
        for odd in range(2):
            for v in range(rows):
                first = pltpu.roll(src[slot(1, odd, v)], half_z, 1)
                last = pltpu.roll(src[slot(half_x, odd, v)], half_z, 1)
                src[slot(0, odd, v)] = jnp.where(upper, last, big_value)
                src[slot(half_x + 1, odd, v)] = jnp.where(upper, big_value, first)

        @pl.loop(0, half_x // FORWARD)
        def _(i):
            for j in range(FORWARD):
                x = i * FORWARD + j
                cur = [[src[slot(x + 1, odd, v)] for v in range(rows)] for odd in range(2)]
                for v in range(rows):
                    for odd in range(2):
                        one = cur[odd][v]
                        pair_z = cur[1 - odd][v]
                        up = y_up(cur[odd], v)
                        down = y_down(cur[odd], v)
                        if v + 1 == rows:
                            up = jnp.where(sub_last, big_value, up)
                        if v == 0:
                            down = jnp.where(sub_first, big_value, down)
                        far_z = jnp.take_along_axis(pair_z, far_index[odd], axis=1)
                        along_x = jnp.minimum(src[slot(x, odd, v)], src[slot(x + 2, odd, v)])
                        low = jnp.minimum(
                            jnp.minimum(along_x, jnp.minimum(up, down)), jnp.minimum(pair_z, far_z)
                        )
                        dst[slot(x + 1, odd, v)] = jnp.minimum(one, low + cost[slot(x, odd, v)])

    assert ITERS % 2 == 0

    @pl.loop(0, ITERS // 2)
    def _(_step):
        sweep(ping, pong)
        sweep(pong, ping)

    @pl.loop(0, half_x)
    def _(x):
        for v in range(rows):
            even, odd = (ping[slot(x + 1, k, v)] - 0.5 * cost[slot(x, k, v)] for k in range(2))
            near, far = swap(even, odd)
            time[(x + 1) * rows + v] = near
            time[(x + half_x + 1) * rows + v] = far

    for v in range(rows):
        time[v] = jnp.full((8, cells_z), -big_value, jnp.float32)
        time[(grid_x + 1) * rows + v] = jnp.full((8, cells_z), -big_value, jnp.float32)

    for load in loads:
        load.wait()

    count = picked.shape[0]
    line = lax.broadcasted_iota(jnp.int32, (1, cells_z), 1)
    unroll = 8

    @pl.loop(0, count // unroll)
    def _(i):
        for j in range(unroll):
            r = pair * count + i * unroll + j
            y = sty_ref[r]
            z = stz_ref[r]
            at = (stx_ref[r] + 1) * rows + (y & (rows - 1))
            got = time[at, pl.ds(y >> shift, 1), :]
            picked[pl.ds(i * unroll + j, 1), :] = jnp.where(line == (z & 1) * half_z + (z >> 1), got, 0.0)

    arrived = jnp.sum(jnp.transpose(picked[...]), axis=0, keepdims=True)
    arr_ref[0] = arrived[:, : count // 2]
    arr_ref[1] = arrived[:, count // 2 :]

    base, length = window(pair_depth, grid_x, ITERS - 1)
    outer, _ = window(pair_depth, grid_x, ITERS)

    def weigh(x, prev, cur):
        nxt = layer_of(time, x + 2)
        spot = (x - base) * rows
        for v in range(rows):
            one = cur[v]

            def gain(other):
                return jnp.maximum(other - one, 0.0)

            up = gain(y_up(cur, v))
            down = gain(y_down(cur, v))
            if v + 1 == rows:
                up = jnp.where(sub_last, 0.0, up)
            if v == 0:
                down = jnp.where(sub_first, 0.0, down)
            parts = (
                gain(prev[v]),
                gain(nxt[v]),
                down,
                up,
                jnp.where(lane_first, 0.0, gain(z_down(one))),
                jnp.where(lane_last, 0.0, gain(z_up(one))),
            )
            total = ((parts[0] + parts[1]) + (parts[2] + parts[3])) + (parts[4] + parts[5])
            inverse = 1.0 / (1.0 + total * (1.0 / spacing))
            scaled = inverse * (1.0 / spacing)
            for k, part in enumerate(parts):
                weight[k, spot + v] = part * scaled
            here = (x - outer) * rows + v
            value = (cnt_ref[here] * one - sum_ref[here]) * inverse
            supply[spot + v] = value
            field[spot + rows + v] = value
        return nxt

    def weigh_body(i, carry):
        prev, cur = carry
        for j in range(2):
            nxt = weigh(base + i * 2 + j, prev, cur)
            prev, cur = cur, nxt
        return prev, cur

    lax.fori_loop(0, length // 2, weigh_body, (layer_of(time, base), layer_of(time, base + 1)))
    for v in range(rows):
        field[v] = jnp.zeros((8, cells_z), jnp.float32)
        field[(length + 1) * rows + v] = jnp.zeros((8, cells_z), jnp.float32)

    def backward(x, prev, cur):
        nxt = layer_of(field, x + 2)
        for v in range(rows):
            one = cur[v]
            spot = x * rows + v
            acc = supply[spot] + weight[0, spot] * prev[v]
            acc = acc + weight[1, spot] * nxt[v]
            side = weight[2, spot] * y_down(cur, v) + weight[3, spot] * y_up(cur, v)
            acc = acc + side
            acc = acc + (weight[4, spot] * z_down(one) + weight[5, spot] * z_up(one))
            field[spot + rows] = acc
        return nxt

    @pl.loop(2, ITERS + 1)
    def _(sweep):
        margin = ITERS - sweep
        span = jnp.minimum(grid_x, (pair_depth + 2 * margin + BACKWARD - 1) // BACKWARD * BACKWARD)
        first = jnp.clip(pair * pair_depth - margin, 0, grid_x - span) - base

        def body(i, carry):
            prev, cur = carry
            for j in range(BACKWARD):
                nxt = backward(first + i * BACKWARD + j, prev, cur)
                prev, cur = cur, nxt
            return prev, cur

        lax.fori_loop(0, span // BACKWARD, body, (layer_of(field, first), layer_of(field, first + 1)))

    mine = pair * pair_depth - base + 1
    for x in range(pair_depth):
        for v in range(rows):
            adj_ref[x, pl.ds(v, 8, stride=rows), :] = jnp.take_along_axis(
                field[(mine + x) * rows + v], join, axis=1
            )


def reduce_kernel(cores, adj_ref, arr_ref, out_ref, got_ref, slots, send_sem, recv_sem, word_send, word_recv):
    depth, keep, _ = out_ref.shape
    brick = lax.axis_index("brick")
    core = lax.axis_index("src")
    parity = lax.rem(brick, 2)
    other = brick + 1 - 2 * parity
    me = core * 2 + parity

    def target(k):
        c = lax.rem(core + k // 2, cores)
        p = lax.rem(parity + k % 2, 2)
        return c, p, brick - parity + p

    def copy(k):
        c, p, b = target(k)
        return remote(
            adj_ref.at[pl.ds(p * depth, depth), pl.ds(c * keep, keep)],
            slots.at[k],
            send_sem.at[k],
            recv_sem.at[k],
            c,
            b,
        )

    barrier = pltpu.get_barrier_semaphore()
    for k in range(1, 2 * cores):
        c, _, b = target(k)
        pl.semaphore_signal(barrier, inc=1, device_id={"src": c, "brick": b}, device_id_type=MESH)
    pl.semaphore_wait(barrier, 2 * cores - 1)
    word = remote(arr_ref.at[1 - parity], got_ref.at[parity], word_send, word_recv, core, other)
    word.start()
    for k in range(1, 2 * cores):
        copy(k).start()
    got_ref[parity] = arr_ref[parity]
    total = adj_ref[pl.ds(parity * depth, depth), pl.ds(pl.multiple_of(core * keep, 8), keep), :]
    for k in range(1, 2 * cores):
        copy(k).wait_recv()
        total = total + slots[k]
    out_ref[...] = total
    for k in range(1, 2 * cores):
        copy(k).wait_send()
    word.wait_send()
    remote(arr_ref.at[parity], got_ref.at[1 - parity], word_send, word_recv, core, other).wait_recv()


def per_device(slowness, source_x, source_y, source_z, station_x, station_y, station_z, observed):
    bricks = lax.axis_size("brick")
    cores = lax.axis_size("src")
    depth, cells_y, cells_z = slowness.shape
    grid_x = depth * bricks
    rec = station_x.shape[0]
    pair_depth = 2 * depth
    rows = cells_y // 8
    assert source_x.shape[0] == 2 and bricks % LOW == 0 and cores % 2 == 0
    f32 = jnp.float32

    wide = min(grid_x, pair_depth + 2 * ITERS)
    field = jax.ShapeDtypeStruct((wide * rows, 8, cells_z), f32)
    full, cnt, total = pl.pallas_call(
        functools.partial(gather_kernel, bricks, pair_depth),
        name="gather",
        out_shape=(jax.ShapeDtypeStruct((grid_x, cells_y, cells_z), f32), field, field),
        in_specs=[VMEM] + [HBM] * 4,
        out_specs=(VMEM, VMEM, VMEM),
        scratch_shapes=[
            pltpu.VMEM((4 * cells_z, rec), jnp.bfloat16),
            pltpu.SemaphoreType.DMA((2, bricks // LOW)),
            pltpu.SemaphoreType.DMA((3, bricks)),
            pltpu.SemaphoreType.DMA((bricks,)),
            pltpu.SemaphoreType.DMA((bricks,)),
            pltpu.SemaphoreType.DMA,
            pltpu.VMEM((1, rec), jnp.int32),
            pltpu.VMEM((1, rec), jnp.int32),
            pltpu.VMEM((1, rec), jnp.int32),
            pltpu.VMEM(observed.shape, f32),
            pltpu.SemaphoreType.DMA((4,)),
        ],
        compiler_params=pltpu.CompilerParams(
            collective_id=0, has_side_effects=True, vmem_limit_bytes=GATHER_VMEM
        ),
    )(slowness, station_x[None], station_y[None], station_z[None], observed)

    length = min(grid_x, pair_depth + 2 * (ITERS - 1))
    share = rec // bricks
    adj, arr = pl.pallas_call(
        functools.partial(solve_kernel, pair_depth),
        name="solve",
        out_shape=(
            jax.ShapeDtypeStruct((pair_depth, cells_y, cells_z), f32),
            jax.ShapeDtypeStruct((2, 1, share), f32),
        ),
        in_specs=[SMEM] * 3 + [HBM] * 3 + [VMEM] * 3,
        out_specs=(VMEM, VMEM),
        scratch_shapes=[
            pltpu.VMEM(((grid_x + 2) * rows, 8, cells_z), f32),
            pltpu.VMEM(((grid_x + 4) * rows, 8, cells_z), f32),
            pltpu.VMEM(((grid_x + 4) * rows, 8, cells_z), f32),
            pltpu.VMEM((grid_x * rows, 8, cells_z), f32),
            pltpu.VMEM((2 * share, cells_z), f32),
            pltpu.VMEM((6, length * rows, 8, cells_z), f32),
            pltpu.VMEM((length * rows, 8, cells_z), f32),
            pltpu.VMEM(((length + 2) * rows, 8, cells_z), f32),
            pltpu.SMEM((rec,), jnp.int32),
            pltpu.SMEM((rec,), jnp.int32),
            pltpu.SMEM((rec,), jnp.int32),
            pltpu.SemaphoreType.DMA((3,)),
        ],
        compiler_params=pltpu.CompilerParams(vmem_limit_bytes=SOLVE_VMEM),
    )(source_x, source_y, source_z, station_x, station_y, station_z, full, cnt, total)

    keep = cells_y // cores
    summed, arrivals = pl.pallas_call(
        functools.partial(reduce_kernel, cores),
        name="reduce",
        out_shape=(
            jax.ShapeDtypeStruct((depth, keep, cells_z), f32),
            jax.ShapeDtypeStruct((2, 1, share), f32),
        ),
        in_specs=[VMEM, VMEM],
        out_specs=(VMEM, VMEM),
        scratch_shapes=[
            pltpu.VMEM((2 * cores, depth, keep, cells_z), f32),
            pltpu.SemaphoreType.DMA((2 * cores,)),
            pltpu.SemaphoreType.DMA((2 * cores,)),
            pltpu.SemaphoreType.DMA,
            pltpu.SemaphoreType.DMA,
        ],
        compiler_params=pltpu.CompilerParams(
            collective_id=1, has_side_effects=True, vmem_limit_bytes=REDUCE_VMEM
        ),
    )(adj, arr)
    own = lax.dynamic_slice_in_dim(slowness, lax.axis_index("src") * keep, keep, axis=1)
    return own * summed, arrivals[:, 0]


def solution(mesh):
    in_specs = (P("brick", None, None), P("src"), P("src"), P("src"), P(), P(), P(), P("src", None))
    out_specs = (P("brick", "src", None), P("src", "brick"))
    return jax.shard_map(
        per_device, mesh=mesh, in_specs=in_specs, out_specs=out_specs, check_vma=False
    )
```
